128 devices in a mesh: shot: 4 (over x_hi, core), gx: 4 (over z), gy: 8 (over x_lo, y).
Axes of the slice: x: 4 (x_hi: 2, x_lo: 2; x = x_hi * 2 + x_lo), y: 4, z: 4, core: 2. Of those that a mesh axis runs over, the one named last changes fastest.
Arguments:
- velocity: bfloat16 [512, 256, 256], P(('shot', 'gx'), 'gy'), may hold values from 0.14941406 to 0.34960938
- epsilon: bfloat16 [512, 256, 256], P(('shot', 'gx'), 'gy'), may hold values from 0.049804688 to 0.29882812
- delta: bfloat16 [512, 256, 256], P(('shot', 'gx'), 'gy'), may hold values from 0.019897461 to 0.14941406
- anchors: int32 [4], replicated, may hold values from 0 to 384
- sources: int32 [4, 3], P('shot'), may hold values from 0 to 255, as said below
- wavelet: float32 [4, 4], P('shot'), may hold values from -8 to 8
- p_now: float32 [4, 128, 256, 256], P('shot', 'gx', 'gy'), may hold values from -6 to 6
- p_prev: float32 [4, 128, 256, 256], P('shot', 'gx', 'gy'), may hold values from -6 to 6
- q_now: float32 [4, 128, 256, 256], P('shot', 'gx', 'gy'), may hold values from -6 to 6
- q_prev: float32 [4, 128, 256, 256], P('shot', 'gx', 'gy'), may hold values from -6 to 6
Outputs:
- p_out: float32 [4, 128, 256, 256], P('shot', 'gx', 'gy')
- q_out: float32 [4, 128, 256, 256], P('shot', 'gx', 'gy')
The draws below stay inside these ranges and needn't reach their ends.
Inputs may be any that keep to these rules, and one draw needn't show every extreme that they name: `sources`: each source lies inside its aperture: x below 128, y below 256, z below 256; some source lies on the aperture's far end along its longest dimension, and some source has x equal to 0.
All inputs are finite; a program needn't handle non-finite values.
Results may differ from the reference program's by a relative error of at most 0.0003.
Values may be sent and summed in bfloat16 or wider, within the bound.
A program may use at most 128 MiB of HBM per device.

```python
import math
import jax
import jax.numpy as jnp
from jax import lax

NZ = 256
STEPS = 4
AX = 128
AY = 256
MX = 512
N_SHOT = 4


def draw_sources(key, part):
    keys = jax.random.split(key, 5)
    largest = max(AX, max(AY, NZ))
    far_shot = jax.random.randint(keys[3], (), 0, N_SHOT)
    near_shot = (far_shot + jax.random.randint(keys[4], (), 1, max(N_SHOT, 2))) % N_SHOT
    shot_ids = jnp.arange(N_SHOT, dtype=jnp.int32)[:, None]
    columns = []
    for column_index, extent in enumerate((AX, AY, NZ)):
        column = jax.random.randint(keys[column_index], (N_SHOT, 1), 0, extent)
        if extent == largest:
            column = jnp.where(shot_ids == far_shot, extent - 1, column)
        if column_index == 0:
            column = jnp.where(shot_ids == near_shot, 0, column)
        columns.append(column)
    return jnp.concatenate(columns, 1).astype(jnp.int32)


def with_ends(entries, rng, least, top_value):
    spot = [jax.random.randint(jax.random.fold_in(rng, axis), (), 0, length) for axis, length in enumerate(entries.shape)]
    main_axis = entries.shape.index(max(entries.shape))
    next_to = spot[:main_axis] + [(spot[main_axis] + 1) % entries.shape[main_axis]] + spot[main_axis + 1:]
    return entries.at[tuple(spot)].set(least).at[tuple(next_to)].set(top_value)


def block_levels(stream_key, dims, cuts, least, high):
    loudness, own = 1.0, jax.random.fold_in(stream_key, 6)
    for dim, parts in cuts:
        draws = jnp.exp(jax.random.uniform(jax.random.fold_in(own, dim), (parts,), jnp.float32, least / len(cuts), high / len(cuts)))
        loudness = loudness * jnp.repeat(draws, dims[dim] // parts).reshape([-1 if axis == dim else 1 for axis in range(len(dims))])
    return loudness


def gaussian(rng, shape, scale, most, cuts=(), kind=jnp.bfloat16):
    loudness = block_levels(rng, shape, cuts, -0.22, 0.18) if cuts else 1.0
    values = jax.random.normal(rng, shape, jnp.float32) * scale * loudness
    return jnp.minimum(jnp.maximum(values, -most), most).astype(kind)


def setup_inputs(seed: int = 0) -> dict:
    arg_keys = jax.random.split(jax.random.key(seed), 11)
    return {
        "velocity": jnp.clip(jnp.exp(math.log(0.34960938) - 0.8500951 * jax.random.uniform(arg_keys[0], (MX, AY, NZ), jnp.float32) ** block_levels(arg_keys[0], (MX, AY, NZ), ((0, 16), (1, 8)), -0.2, 0.2)), 0.14941406, 0.34960938).astype(jnp.bfloat16),
        "epsilon": jnp.clip(jnp.exp(math.log(0.29882812) - 1.7917595 * jax.random.uniform(arg_keys[1], (MX, AY, NZ), jnp.float32) ** block_levels(arg_keys[1], (MX, AY, NZ), ((0, 16), (1, 8)), -0.2, 0.2)), 0.049804688, 0.29882812).astype(jnp.bfloat16),
        "delta": jnp.clip(jnp.exp(math.log(0.14941406) - 2.0161293 * jax.random.uniform(arg_keys[2], (MX, AY, NZ), jnp.float32) ** block_levels(arg_keys[2], (MX, AY, NZ), ((0, 16), (1, 8)), -0.2, 0.2)), 0.019897461, 0.14941406).astype(jnp.bfloat16),
        "anchors": with_ends(jax.random.randint(arg_keys[3], (N_SHOT,), 0, MX - AX + 1), jax.random.fold_in(arg_keys[3], 1), 0, MX - AX).astype(jnp.int32),
        "sources": draw_sources(jax.random.fold_in(arg_keys[10], 71), 0),
        "wavelet": gaussian(arg_keys[5], (N_SHOT, STEPS), 2.0, 8.0, ((0, 4),), jnp.float32),
        "p_now": gaussian(arg_keys[6], (N_SHOT, AX, AY, NZ), 1.0, 6.0, ((0, 4), (1, 4), (2, 8)), jnp.float32),
        "p_prev": gaussian(arg_keys[7], (N_SHOT, AX, AY, NZ), 1.0, 6.0, ((0, 4), (1, 4), (2, 8)), jnp.float32),
        "q_now": gaussian(arg_keys[8], (N_SHOT, AX, AY, NZ), 1.0, 6.0, ((0, 4), (1, 4), (2, 8)), jnp.float32),
        "q_prev": gaussian(arg_keys[9], (N_SHOT, AX, AY, NZ), 1.0, 6.0, ((0, 4), (1, 4), (2, 8)), jnp.float32),
    }


STENCIL_WEIGHTS = (-205.0 / 72.0, 8.0 / 5.0, -1.0 / 5.0, 8.0 / 315.0, -1.0 / 560.0)

def shifted_up(values, reach):
    filler = jnp.zeros(values.shape[:-1] + (reach,), values.dtype)
    return jnp.concatenate([values[..., reach:], filler], -1)

def shifted_down(values, reach):
    filler = jnp.zeros(values.shape[:-1] + (reach,), values.dtype)
    return jnp.concatenate([filler, values[..., :-reach]], -1)

def vertical_second(values):
    total = STENCIL_WEIGHTS[0] * values
    for reach in range(1, 5):
        total = total + STENCIL_WEIGHTS[reach] * (shifted_up(values, reach) + shifted_down(values, reach))
    return total

def horizontal_second(padded, x_count, y_count):
    x_total = STENCIL_WEIGHTS[0] * padded[4:4 + x_count, 4:4 + y_count]
    for reach in range(1, 5):
        x_total = x_total + STENCIL_WEIGHTS[reach] * (padded[4 + reach:4 + reach + x_count, 4:4 + y_count] + padded[4 - reach:4 - reach + x_count, 4:4 + y_count])
    y_total = STENCIL_WEIGHTS[0] * padded[4:4 + x_count, 4:4 + y_count]
    for reach in range(1, 5):
        y_total = y_total + STENCIL_WEIGHTS[reach] * (padded[4:4 + x_count, 4 + reach:4 + reach + y_count] + padded[4:4 + x_count, 4 - reach:4 - reach + y_count])
    return x_total + y_total

def update(padded_p, p_field, p_before, q_field, q_before, courant_sq, horiz_gain, cross_gain):
    laplace_h = horizontal_second(padded_p, p_field.shape[0], p_field.shape[1])
    depth_term = vertical_second(q_field)
    p_next = 2.0 * p_field - p_before + courant_sq * (horiz_gain * laplace_h + cross_gain * depth_term)
    q_next = 2.0 * q_field - q_before + courant_sq * (cross_gain * laplace_h + depth_term)
    return (p_next, q_next)

def reference(velocity, epsilon, delta, anchors, sources, wavelet, p_now, p_prev, q_now, q_prev):
    results_p = []
    results_q = []
    for shot_group in range(N_SHOT):
        anchor_row = anchors[shot_group].astype(jnp.int32)
        velocity_block = lax.dynamic_slice_in_dim(velocity, anchor_row, AX, 0).astype(jnp.float32)
        epsilon_block = lax.dynamic_slice_in_dim(epsilon, anchor_row, AX, 0).astype(jnp.float32)
        delta_block = lax.dynamic_slice_in_dim(delta, anchor_row, AX, 0).astype(jnp.float32)
        courant_sq = velocity_block * velocity_block
        horiz_gain = 1.0 + 2.0 * epsilon_block
        cross_gain = jnp.sqrt(1.0 + 2.0 * delta_block)
        p_field = p_now[shot_group]
        p_before = p_prev[shot_group]
        q_field = q_now[shot_group]
        q_before = q_prev[shot_group]
        for step_index in range(STEPS):
            padded = jnp.pad(p_field, ((4, 4), (4, 4), (0, 0)))
            p_next, q_next = update(padded, p_field, p_before, q_field, q_before, courant_sq, horiz_gain, cross_gain)
            p_next = p_next.at[sources[shot_group, 0], sources[shot_group, 1], sources[shot_group, 2]].add(wavelet[shot_group, step_index])
            p_before, p_field, q_before, q_field = (p_field, p_next, q_field, q_next)
        results_p.append(p_field)
        results_q.append(q_field)
    return (jnp.stack(results_p), jnp.stack(results_q))
```

```python
import jax
import jax.numpy as jnp
from jax import lax
from jax.experimental import pallas as pl
from jax.experimental.pallas import tpu as pltpu
from jax.sharding import PartitionSpec as P

STEPS = 4
WEIGHTS = (-205.0 / 72.0, 8.0 / 5.0, -1.0 / 5.0, 8.0 / 315.0, -1.0 / 560.0)
MESH = pl.DeviceIdType.MESH
N = 32
ROWS = (2, 2, 2, 2)
FIRST = (0, 2, 4, 6)
CHUNKS = len(ROWS)
HOPS = (1, 3, 2)


def kernel(
    velocity, epsilon, delta, anchors, sources, wavelet, p_now, p_prev, q_now, q_prev,
    p_out, q_out,
    slab, gathered0, gathered1, gathered2, gathered3, outgoing, window,
    gain_a, gain_b, gain_c, lap, deep, band_hi, band_lo, spot,
    p_m, p_0, p_1, p_2, p_3, p_4, q_m, q_0, q_1, q_2, q_3, q_4,
    rim_out, rim_in,
    load_sem, spread_send, spread_recv, own_sem, x_send, x_recv, core_send, core_recv,
    deal_send, deal_recv, halo_send, halo_recv, store_sem,
):
    gathered = (gathered0, gathered1, gathered2, gathered3)
    p = (p_0, p_1, p_2, p_3, p_4)
    q = (q_0, q_1, q_2, q_3, q_4)
    shot = lax.axis_index("shot")
    gx = lax.axis_index("gx")
    gy = lax.axis_index("gy")
    far = lax.rem(shot + 2, 4)
    mate = shot + 1 - 2 * lax.rem(shot, 2)
    far_mate = lax.rem(mate + 2, 4)
    has_gx = (gx > 0, gx < 3)
    has_gy = (gy > 0, gy < 7)

    def to(s, z, y):
        return (s, z, y)

    barrier = pltpu.get_barrier_semaphore()
    for hop in HOPS:
        pl.semaphore_signal(barrier, inc=1, device_id=to(shot, lax.rem(gx + hop, 4), gy), device_id_type=MESH)
    pl.semaphore_signal(barrier, inc=1, device_id=to(far, gx, gy), device_id_type=MESH)
    pl.semaphore_signal(barrier, inc=1, device_id=to(mate, gx, gy), device_id_type=MESH)
    for side in range(2):
        @pl.when(has_gy[side])
        def _():
            pl.semaphore_signal(barrier, inc=1, device_id=to(shot, gx, gy + 2 * side - 1), device_id_type=MESH)

    loads = []
    def load(src, dst):
        copy = pltpu.make_async_copy(src, dst, load_sem.at[len(loads)])
        copy.start()
        loads.append(copy)
    for m, model in enumerate((velocity, epsilon, delta)):
        load(model, slab.at[m])
    for half in range(2):
        z = pl.ds(128 * half, 128)
        load(p_now.at[0, :, :, z], p_0.at[pl.ds(4, N), half, pl.ds(8, N), :])
    for src, dst in ((p_prev, p_m), (q_now, q_0), (q_prev, q_m)):
        for half in range(2):
            load(src.at[0, :, :, pl.ds(128 * half, 128)], dst.at[:, half])

    pl.semaphore_wait(barrier, 5 + has_gy[0].astype(jnp.int32) + has_gy[1].astype(jnp.int32))

    for m in range(3):
        loads[m].wait()
    spread = {}
    x_copy = {}
    for c in range(CHUNKS):
        for d, hop in enumerate(HOPS):
            z = lax.rem(gx + hop, 4)
            spread[c, d] = pltpu.make_async_remote_copy(
                src_ref=slab.at[:, pl.ds(8 * z + FIRST[c], ROWS[c])],
                dst_ref=gathered[c].at[shot, gx],
                send_sem=spread_send.at[c, d], recv_sem=spread_recv.at[c, d],
                device_id=to(shot, z, gy), device_id_type=MESH)
            spread[c, d].start()
        own_rows = slab.at[:, pl.ds(8 * gx + FIRST[c], ROWS[c])]
        x_copy[c, 0] = pltpu.make_async_remote_copy(
            src_ref=own_rows, dst_ref=gathered[c].at[shot, gx],
            send_sem=x_send.at[c, 0], recv_sem=x_recv.at[c, 0],
            device_id=to(far, gx, gy), device_id_type=MESH)
        x_copy[c, 0].start()
    own = []
    for c in range(CHUNKS):
        own.append(pltpu.make_async_copy(
            slab.at[:, pl.ds(8 * gx + FIRST[c], ROWS[c])], gathered[c].at[shot, gx], own_sem.at[c]))
        own[c].start()

    def x_halo(t, side):
        return pltpu.make_async_remote_copy(
            src_ref=p[t].at[pl.ds(4 if side == 0 else 32, 4), :, pl.ds(8, N), :],
            dst_ref=p[t].at[pl.ds(36 if side == 0 else 0, 4), :, pl.ds(8, N), :],
            send_sem=halo_send.at[t, side], recv_sem=halo_recv.at[t, side],
            device_id=to(shot, gx + 2 * side - 1, gy), device_id_type=MESH)

    def y_halo(t, side):
        return pltpu.make_async_remote_copy(
            src_ref=rim_out.at[t, side], dst_ref=rim_in.at[t, 1 - side],
            send_sem=halo_send.at[t, 2 + side], recv_sem=halo_recv.at[t, 2 + side],
            device_id=to(shot, gx, gy + 2 * side - 1), device_id_type=MESH)

    def send_x(t):
        for side in range(2):
            @pl.when(has_gx[side])
            def _():
                x_halo(t, side).start()

    def send_y(t):
        for side in range(2):
            @pl.when(has_gy[side])
            def _():
                y_halo(t, side).start()

    def await_halos(t):
        for side in range(2):
            @pl.when(has_gx[side])
            def _():
                x_halo(t, 1 - side).wait_recv()
                x_halo(t, side).wait_send()
        for side in range(2):
            @pl.when(has_gy[side])
            def _():
                y_halo(t, 1 - side).wait_recv()
                y_halo(t, side).wait_send()

            @pl.when(jnp.logical_not(has_gy[side]))
            def _():
                rim_in[t, side] = jnp.zeros((N, 2, 4, 128), jnp.float32)

        @pl.loop(0, N)
        def _(x):
            for half in range(2):
                p[t][x + 4, half, 4:8, :] = rim_in[t, 0, x, half]
                p[t][x + 4, half, 40:44, :] = rim_in[t, 1, x, half]

    for side in range(2):
        @pl.when(jnp.logical_not(has_gx[side]))
        def _():
            for t in range(STEPS):
                @pl.loop(0, 4)
                def _(x):
                    for half in range(2):
                        p[t][x + 36 * side, half, 8:40, :] = jnp.zeros((N, 128), jnp.float32)

    row = lax.broadcasted_iota(jnp.int32, (256, 256), 0)
    col = lax.broadcasted_iota(jnp.int32, (256, 256), 1)
    apart = jnp.abs(row - col)
    band = jnp.zeros((256, 256), jnp.float32)
    for k in range(5):
        band = jnp.where(apart == k, jnp.float32(WEIGHTS[k]), band)
    hi = band.astype(jnp.bfloat16)
    band_hi[...] = hi
    band_lo[...] = (band - hi.astype(jnp.float32)).astype(jnp.bfloat16)
    y_at = lax.broadcasted_iota(jnp.int32, (N, 128), 0) + gy * N
    z_at = lax.broadcasted_iota(jnp.int32, (N, 128), 1)
    for half in range(2):
        here = jnp.logical_and(y_at == sources[0, 1], z_at + 128 * half == sources[0, 2])
        spot[half] = jnp.where(here, jnp.float32(1), jnp.float32(0))

    for i in range(3, 5):
        loads[i].wait()

    @pl.loop(0, N)
    def _(x):
        for half in range(2):
            rim_out[0, 0, x, half] = p_0[x + 4, half, 8:12, :]
            rim_out[0, 1, x, half] = p_0[x + 4, half, 36:40, :]
    send_x(0)
    send_y(0)

    core_copy = {}

    def core(c, which, s):
        core_copy[c, which] = pltpu.make_async_remote_copy(
            src_ref=gathered[c].at[s], dst_ref=gathered[c].at[s],
            send_sem=core_send.at[c, which], recv_sem=core_recv.at[c, which],
            device_id=to(mate, gx, gy), device_id_type=MESH)
        core_copy[c, which].start()

    def forward(c):
        for d, hop in enumerate(HOPS):
            spread[c, d].wait_recv()
            z = lax.rem(gx + 4 - hop, 4)
            x_copy[c, d + 1] = pltpu.make_async_remote_copy(
                src_ref=gathered[c].at[shot, z], dst_ref=gathered[c].at[shot, z],
                send_sem=x_send.at[c, d + 1], recv_sem=x_recv.at[c, d + 1],
                device_id=to(far, gx, gy), device_id_type=MESH)
            x_copy[c, d + 1].start()
        own[c].wait()
        core(c, 0, shot)

    forward(0)
    forward(1)

    def depth_term(t):
        @pl.loop(0, N // 4)
        def _(group):
            x = 4 * group
            values = jnp.concatenate(
                [q[t][pl.ds(x, 4), 0].reshape(4 * N, 128), q[t][pl.ds(x, 4), 1].reshape(4 * N, 128)], axis=-1)
            hi = values.astype(jnp.bfloat16)
            lo = (values - hi.astype(jnp.float32)).astype(jnp.bfloat16)
            total = jnp.dot(hi, band_hi[...], preferred_element_type=jnp.float32)
            total = total + jnp.dot(lo, band_hi[...], preferred_element_type=jnp.float32)
            total = total + jnp.dot(hi, band_lo[...], preferred_element_type=jnp.float32)
            deep[pl.ds(x, 4), 0] = total[:, :128].reshape(4, N, 128)
            deep[pl.ds(x, 4), 1] = total[:, 128:].reshape(4, N, 128)

    def laplace(t, x, half):
        total = (2.0 * WEIGHTS[0]) * p[t][x + 4, half, 8:40, :]
        for k in range(1, 5):
            pair = p[t][x + 4 + k, half, 8:40, :] + p[t][x + 4 - k, half, 8:40, :]
            pair = pair + (p[t][x + 4, half, 8 + k:40 + k, :] + p[t][x + 4, half, 8 - k:40 - k, :])
            total = total + WEIGHTS[k] * pair
        return total

    for i in range(5, len(loads)):
        loads[i].wait()
    depth_term(0)
    await_halos(0)

    @pl.loop(0, N)
    def _(x):
        for half in range(2):
            lap[x, half] = laplace(0, x, half)

    for c in range(2, CHUNKS):
        forward(c)

    anchor = anchors[shot]
    shift = lax.rem(anchor, N)
    base = lax.div(anchor, N)
    deal = {}

    def select(c):
        for d in (0, 1, 3, 2):
            x_copy[c, d].wait_recv()
        core(c, 1, far)
        core_copy[c, 0].wait_recv()
        core_copy[c, 1].wait_recv()
        for d, hop in enumerate(HOPS + (0,)):
            z = lax.rem(gx + hop, 4)
            for kk in range(ROWS[c]):
                k = 8 * gx + FIRST[c] + kk
                at = jnp.minimum(base + z + (k < shift).astype(jnp.int32), 15)
                values = gathered[c][lax.div(at, 4), lax.rem(at, 4), :, kk]
                if hop:
                    outgoing[d, :, FIRST[c] + kk] = values
                else:
                    window[:, gx, FIRST[c] + kk] = values
            if hop:
                deal[c, d] = pltpu.make_async_remote_copy(
                    src_ref=outgoing.at[d, :, pl.ds(FIRST[c], ROWS[c])],
                    dst_ref=window.at[:, gx, pl.ds(FIRST[c], ROWS[c])],
                    send_sem=deal_send.at[c, d], recv_sem=deal_recv.at[c, d],
                    device_id=to(shot, z, gy), device_id_type=MESH)
                deal[c, d].start()

    def gains(c):
        for d in range(3):
            deal[c, d].wait_recv()

        @pl.loop(0, 4)
        def _(block):
            for kk in range(FIRST[c], FIRST[c] + ROWS[c]):
                speed = window[0, block, kk].astype(jnp.float32)
                eps = window[1, block, kk].astype(jnp.float32)
                dlt = window[2, block, kk].astype(jnp.float32)
                square = speed * speed
                cross = square * jnp.sqrt(1.0 + 2.0 * dlt)
                horiz = square * (1.0 + 2.0 * eps)
                for half in range(2):
                    z = slice(128 * half, 128 * half + 128)
                    gain_a[8 * block + kk, half] = horiz[:, z]
                    gain_b[8 * block + kk, half] = cross[:, z]
                    gain_c[8 * block + kk, half] = square[:, z]

    select(0)
    for c in range(1, CHUNKS):
        select(c)
        gains(c - 1)
    gains(CHUNKS - 1)

    def step(t):
        before_p = p_m if t == 0 else p[t - 1]
        before_q = q_m if t == 0 else q[t - 1]
        off = 0 if t == 0 else 4
        y0 = 0 if t == 0 else 8
        last = t == STEPS - 1

        @pl.loop(0, N)
        def _(x):
            k = lax.rem(x + shift, N)
            amount = jnp.where(x + gx * N == sources[0, 0], wavelet[0, t], jnp.float32(0))
            for half in range(2):
                h = lap[x, half] if t == 0 else laplace(t, x, half)
                z = deep[x, half]
                a, b, c = gain_a[k, half], gain_b[k, half], gain_c[k, half]
                new_p = (2.0 * p[t][x + 4, half, 8:40, :] - before_p[x + off, half, y0:y0 + N, :]) + (a * h + b * z)
                new_p = new_p + amount * spot[half]
                new_q = (2.0 * q[t][x, half] - before_q[x, half]) + (b * h + c * z)
                q[t + 1][x, half] = new_q
                if last:
                    p[t + 1][x, half] = new_p
                else:
                    p[t + 1][x + 4, half, 8:40, :] = new_p
                    rim_out[t + 1, 0, x, half] = new_p[0:4]
                    rim_out[t + 1, 1, x, half] = new_p[28:32]

    for t in range(STEPS):
        if t > 0:
            depth_term(t)
            await_halos(t)
        step(t)
        if t < STEPS - 1:
            send_x(t + 1)
            send_y(t + 1)

    stores = []
    for src, dst in ((p_4, p_out), (q_4, q_out)):
        for half in range(2):
            stores.append(pltpu.make_async_copy(
                src.at[:, half], dst.at[0, :, :, pl.ds(128 * half, 128)], store_sem.at[len(stores)]))
            stores[-1].start()
    for c in range(CHUNKS):
        for d in range(3):
            spread[c, d].wait_send()
            deal[c, d].wait_send()
        for d in range(4):
            x_copy[c, d].wait_send()
        core_copy[c, 0].wait_send()
        core_copy[c, 1].wait_send()
    for copy in stores:
        copy.wait()


def on_device(velocity, epsilon, delta, anchors, sources, wavelet, p_now, p_prev, q_now, q_prev):
    out = jax.ShapeDtypeStruct(p_now.shape, jnp.float32)
    hbm = pl.BlockSpec(memory_space=pl.ANY)
    smem = pl.BlockSpec(memory_space=pltpu.SMEM)
    f32 = jnp.float32
    bf16 = jnp.bfloat16
    block = pltpu.VMEM((N, 2, N, 128), f32)
    padded = pltpu.VMEM((N + 8, 2, N + 16, 128), f32)
    dma = pltpu.SemaphoreType.DMA
    return pl.pallas_call(
        kernel,
        out_shape=(out, out),
        in_specs=[hbm, hbm, hbm, smem, smem, smem, hbm, hbm, hbm, hbm],
        out_specs=(hbm, hbm),
        scratch_shapes=[
            pltpu.VMEM((3, N, N, 256), bf16),
            *[pltpu.VMEM((4, 4, 3, rows, N, 256), bf16) for rows in ROWS],
            pltpu.VMEM((3, 3, 8, N, 256), bf16),
            pltpu.VMEM((3, 4, 8, N, 256), bf16),
            block, block, block, block, block,
            pltpu.VMEM((256, 256), bf16), pltpu.VMEM((256, 256), bf16), pltpu.VMEM((2, N, 128), f32),
            block, padded, padded, padded, padded, block,
            block, block, block, block, block, block,
            pltpu.VMEM((STEPS, 2, N, 2, 4, 128), f32), pltpu.VMEM((STEPS, 2, N, 2, 4, 128), f32),
            dma((11,)), dma((CHUNKS, 3)), dma((CHUNKS, 3)), dma((CHUNKS,)), dma((CHUNKS, 4)), dma((CHUNKS, 4)),
            dma((CHUNKS, 2)), dma((CHUNKS, 2)), dma((CHUNKS, 3)), dma((CHUNKS, 3)),
            dma((STEPS, 4)), dma((STEPS, 4)), dma((4,)),
        ],
        compiler_params=pltpu.CompilerParams(
            collective_id=0, has_side_effects=True, vmem_limit_bytes=56 << 20),
        name="migrate",
    )(velocity, epsilon, delta, anchors, sources, wavelet, p_now, p_prev, q_now, q_prev)


def solution(mesh):
    field = P("shot", "gx", "gy", None)
    model = P(("shot", "gx"), "gy", None)
    return jax.shard_map(
        on_device,
        mesh=mesh,
        in_specs=(model, model, model, P(), P("shot", None), P("shot", None), field, field, field, field),
        out_specs=(field, field),
        check_vma=False,
    )
```

```python
import jax
import jax.numpy as jnp
from jax import lax
from jax.experimental import pallas as pl
from jax.experimental.pallas import tpu as pltpu
from jax.sharding import PartitionSpec as P

STEPS = 4
WEIGHTS = (-205.0 / 72.0, 8.0 / 5.0, -1.0 / 5.0, 8.0 / 315.0, -1.0 / 560.0)
MESH = pl.DeviceIdType.MESH
N = 32
ROWS = (2, 2, 2, 1, 1)
FIRST = tuple(sum(ROWS[:c]) for c in range(len(ROWS)))
CHUNKS = len(ROWS)
HOPS = (1, 3, 2)


def kernel(
    velocity, epsilon, delta, anchors, sources, wavelet, p_now, p_prev, q_now, q_prev,
    p_out, q_out,
    slab, *scratch,
):
    gathered = scratch[:CHUNKS]
    (outgoing, window,
    gain_a, gain_b, gain_c, lap, deep, band_hi, band_lo, spot,
    p_m, p_0, p_1, p_2, p_3, q_m, q_0, q_1, q_2, q_3,
    stage, corner, x_out, x_in, y_out, y_in,
    load_sem, spread_send, spread_recv, own_sem, x_send, x_recv, core_send, core_recv,
    deal_send, deal_recv, halo_send, halo_recv) = scratch[CHUNKS:]
    p = (p_0, p_1, p_2, p_3)
    q = (q_0, q_1, q_2, q_3)
    shot = lax.axis_index("shot")
    gx = lax.axis_index("gx")
    gy = lax.axis_index("gy")
    far = lax.rem(shot + 2, 4)
    mate = shot + 1 - 2 * lax.rem(shot, 2)
    far_mate = lax.rem(mate + 2, 4)
    has_gx = (gx > 0, gx < 3)
    has_gy = (gy > 0, gy < 7)

    def to(s, z, y):
        return (s, z, y)

    barrier = pltpu.get_barrier_semaphore()
    for hop in HOPS:
        pl.semaphore_signal(barrier, inc=1, device_id=to(shot, lax.rem(gx + hop, 4), gy), device_id_type=MESH)
    pl.semaphore_signal(barrier, inc=1, device_id=to(far, gx, gy), device_id_type=MESH)
    pl.semaphore_signal(barrier, inc=1, device_id=to(mate, gx, gy), device_id_type=MESH)
    for side in range(2):
        @pl.when(has_gy[side])
        def _():
            pl.semaphore_signal(barrier, inc=1, device_id=to(shot, gx, gy + 2 * side - 1), device_id_type=MESH)

    loads = []
    def load(src, dst):
        copy = pltpu.make_async_copy(src, dst, load_sem.at[len(loads)])
        copy.start()
        loads.append(copy)
    for m, model in enumerate((velocity, epsilon, delta)):
        load(model, slab.at[m])
    for half in range(2):
        z = pl.ds(128 * half, 128)
        load(p_now.at[0, :, :, z], p_0.at[pl.ds(4, N), half, pl.ds(8, N), :])
    for src, dst in ((p_prev, p_m), (q_now, q_0), (q_prev, q_m)):
        for half in range(2):
            load(src.at[0, :, :, pl.ds(128 * half, 128)], dst.at[:, half])

    pl.semaphore_wait(barrier, 5 + has_gy[0].astype(jnp.int32) + has_gy[1].astype(jnp.int32))

    for m in range(3):
        loads[m].wait()
    spread = {}
    x_copy = {}
    def scatter(c):
        for d, hop in enumerate(HOPS):
            z = lax.rem(gx + hop, 4)
            spread[c, d] = pltpu.make_async_remote_copy(
                src_ref=slab.at[:, pl.ds(8 * z + FIRST[c], ROWS[c])],
                dst_ref=gathered[c].at[shot, gx],
                send_sem=spread_send.at[c, d], recv_sem=spread_recv.at[c, d],
                device_id=to(shot, z, gy), device_id_type=MESH)
            spread[c, d].start()

    def cross_own(c):
        own_rows = slab.at[:, pl.ds(8 * gx + FIRST[c], ROWS[c])]
        x_copy[c, 0] = pltpu.make_async_remote_copy(
            src_ref=own_rows, dst_ref=gathered[c].at[shot, gx],
            send_sem=x_send.at[c, 0], recv_sem=x_recv.at[c, 0],
            device_id=to(far, gx, gy), device_id_type=MESH)
        x_copy[c, 0].start()

    for c in range(CHUNKS):
        scatter(c)
        cross_own(c)
    own = []
    for c in range(CHUNKS):
        own.append(pltpu.make_async_copy(
            slab.at[:, pl.ds(8 * gx + FIRST[c], ROWS[c])], gathered[c].at[shot, gx], own_sem.at[c]))
        own[c].start()

    def x_halo(t, side):
        return pltpu.make_async_remote_copy(
            src_ref=x_out.at[t, side], dst_ref=x_in.at[t, 1 - side],
            send_sem=halo_send.at[t, side], recv_sem=halo_recv.at[t, side],
            device_id=to(shot, gx + 2 * side - 1, gy), device_id_type=MESH)

    def y_halo(t, side):
        return pltpu.make_async_remote_copy(
            src_ref=y_out.at[t, side], dst_ref=y_in.at[t, 1 - side],
            send_sem=halo_send.at[t, 2 + side], recv_sem=halo_recv.at[t, 2 + side],
            device_id=to(shot, gx, gy + 2 * side - 1), device_id_type=MESH)

    def pack_layers(out, side, layer, half, values):
        near = 3 if side else 0
        hi = values.astype(jnp.bfloat16)
        out[layer, half] = hi
        if layer == near:
            out[4, half] = (values - hi.astype(jnp.float32)).astype(jnp.bfloat16)

    def unpack_layers(source, side, half):
        near = 0 if side else 3
        layers = [source[layer, half].astype(jnp.float32) for layer in range(4)]
        layers[near] = layers[near] + source[4, half].astype(jnp.float32)
        return layers

    def corrections(layers, side):
        result = []
        for i in range(4):
            reach = range(i + 1) if side else range(i, 4)
            terms = [WEIGHTS[4 + j - i if side else i + 4 - j] * layers[j] for j in reach]
            total = terms[0]
            for term in terms[1:]:
                total = total + term
            result.append(total)
        return result

    def send_rims(t):
        for side in range(2):
            for half in range(2):
                for layer in range(4):
                    pack_layers(x_out.at[t, side], side, layer, half, p[t][4 + 28 * side + layer, half, 8:40, :])
            @pl.when(has_gx[side])
            def _():
                x_halo(t, side).start()
        for side in range(2):
            for half in range(2):
                for layer in range(4):
                    pack_layers(y_out.at[t, side], side, layer, half, stage[side, half, N * layer:N * layer + N, :])
            @pl.when(has_gy[side])
            def _():
                y_halo(t, side).start()

    def await_halos(t):
        for side in range(2):
            @pl.when(has_gx[side])
            def _():
                x_halo(t, 1 - side).wait_recv()
                x_halo(t, side).wait_send()
        for side in range(2):
            @pl.when(has_gy[side])
            def _():
                y_halo(t, 1 - side).wait_recv()
                y_halo(t, side).wait_send()

    def y_corrections(t):
        for side in range(2):
            for half in range(2):
                for i, value in enumerate(corrections(unpack_layers(y_in.at[t, side], side, half), side)):
                    corner[side, half, N * i:N * i + N, :] = value

    for side in range(2):
        @pl.when(jnp.logical_not(has_gx[side]))
        def _():
            for t in range(STEPS):
                x_in[t, side] = jnp.zeros((5, 2, N, 128), jnp.bfloat16)

        @pl.when(jnp.logical_not(has_gy[side]))
        def _():
            for t in range(STEPS):
                y_in[t, side] = jnp.zeros((5, 2, N, 128), jnp.bfloat16)

    for t in range(STEPS):
        @pl.loop(0, 4)
        def _(x):
            for half in range(2):
                p[t][x, half, 8:40, :] = jnp.zeros((N, 128), jnp.float32)
                p[t][x + 36, half, 8:40, :] = jnp.zeros((N, 128), jnp.float32)

        @pl.loop(0, N)
        def _(x):
            for half in range(2):
                p[t][x + 4, half, 0:8, :] = jnp.zeros((8, 128), jnp.float32)
                p[t][x + 4, half, 40:48, :] = jnp.zeros((8, 128), jnp.float32)

    row = lax.broadcasted_iota(jnp.int32, (256, 256), 0)
    col = lax.broadcasted_iota(jnp.int32, (256, 256), 1)
    apart = jnp.abs(row - col)
    band = jnp.zeros((256, 256), jnp.float32)
    for k in range(5):
        band = jnp.where(apart == k, jnp.float32(WEIGHTS[k]), band)
    hi = band.astype(jnp.bfloat16)
    band_hi[...] = hi
    band_lo[...] = (band - hi.astype(jnp.float32)).astype(jnp.bfloat16)
    y_at = lax.broadcasted_iota(jnp.int32, (N, 128), 0) + gy * N
    z_at = lax.broadcasted_iota(jnp.int32, (N, 128), 1)
    for half in range(2):
        here = jnp.logical_and(y_at == sources[0, 1], z_at + 128 * half == sources[0, 2])
        spot[half] = jnp.where(here, jnp.float32(1), jnp.float32(0))

    for i in range(3, 5):
        loads[i].wait()

    @pl.loop(0, N)
    def _(x):
        for half in range(2):
            stage[0, half, pl.ds(x, 4, stride=N), :] = p_0[x + 4, half, 8:12, :]
            stage[1, half, pl.ds(x, 4, stride=N), :] = p_0[x + 4, half, 36:40, :]
    send_rims(0)

    core_copy = {}

    def core(c, which, s):
        core_copy[c, which] = pltpu.make_async_remote_copy(
            src_ref=gathered[c].at[s], dst_ref=gathered[c].at[s],
            send_sem=core_send.at[c, which], recv_sem=core_recv.at[c, which],
            device_id=to(mate, gx, gy), device_id_type=MESH)
        core_copy[c, which].start()

    def forward(c):
        for d, hop in enumerate(HOPS):
            spread[c, d].wait_recv()
            z = lax.rem(gx + 4 - hop, 4)
            x_copy[c, d + 1] = pltpu.make_async_remote_copy(
                src_ref=gathered[c].at[shot, z], dst_ref=gathered[c].at[shot, z],
                send_sem=x_send.at[c, d + 1], recv_sem=x_recv.at[c, d + 1],
                device_id=to(far, gx, gy), device_id_type=MESH)
            x_copy[c, d + 1].start()
        own[c].wait()
        core(c, 0, shot)


    def depth_term(t):
        values = jnp.concatenate([q[t][:, 0].reshape(N * N, 128), q[t][:, 1].reshape(N * N, 128)], axis=-1)
        hi = values.astype(jnp.bfloat16)
        lo = (values - hi.astype(jnp.float32)).astype(jnp.bfloat16)
        total = jnp.dot(hi, band_hi[...], preferred_element_type=jnp.float32)
        total = total + jnp.dot(lo, band_hi[...], preferred_element_type=jnp.float32)
        total = total + jnp.dot(hi, band_lo[...], preferred_element_type=jnp.float32)
        deep[:, 0] = total[:, :128].reshape(N, N, 128)
        deep[:, 1] = total[:, 128:].reshape(N, N, 128)

    def laplace(t, x, half):
        total = (2.0 * WEIGHTS[0]) * p[t][x + 4, half, 8:40, :]
        for k in range(1, 5):
            pair = p[t][x + 4 + k, half, 8:40, :] + p[t][x + 4 - k, half, 8:40, :]
            pair = pair + (p[t][x + 4, half, 8 + k:40 + k, :] + p[t][x + 4, half, 8 - k:40 - k, :])
            total = total + WEIGHTS[k] * pair
        return total

    anchor = anchors[shot]
    shift = lax.rem(anchor, N)
    base = lax.div(anchor, N)
    deal = {}

    def select(c):
        for d in (0, 1, 3, 2):
            x_copy[c, d].wait_recv()
        core(c, 1, far)
        core_copy[c, 0].wait_recv()
        core_copy[c, 1].wait_recv()
        for d, hop in enumerate(HOPS + (0,)):
            z = lax.rem(gx + hop, 4)
            for kk in range(ROWS[c]):
                k = 8 * gx + FIRST[c] + kk
                at = jnp.minimum(base + z + (k < shift).astype(jnp.int32), 15)
                values = gathered[c][lax.div(at, 4), lax.rem(at, 4), :, kk]
                if hop:
                    outgoing[d, :, FIRST[c] + kk] = values
                else:
                    window[:, gx, FIRST[c] + kk] = values
            if hop:
                deal[c, d] = pltpu.make_async_remote_copy(
                    src_ref=outgoing.at[d, :, pl.ds(FIRST[c], ROWS[c])],
                    dst_ref=window.at[:, gx, pl.ds(FIRST[c], ROWS[c])],
                    send_sem=deal_send.at[c, d], recv_sem=deal_recv.at[c, d],
                    device_id=to(shot, z, gy), device_id_type=MESH)
                deal[c, d].start()

    def gains(c):
        for d in range(3):
            deal[c, d].wait_recv()

        @pl.loop(0, 4)
        def _(block):
            for kk in range(FIRST[c], FIRST[c] + ROWS[c]):
                speed = window[0, block, kk].astype(jnp.float32)
                eps = window[1, block, kk].astype(jnp.float32)
                dlt = window[2, block, kk].astype(jnp.float32)
                square = speed * speed
                cross = square * jnp.sqrt(1.0 + 2.0 * dlt)
                horiz = square * (1.0 + 2.0 * eps)
                for half in range(2):
                    z = slice(128 * half, 128 * half + 128)
                    gain_a[8 * block + kk, half] = horiz[:, z]
                    gain_b[8 * block + kk, half] = cross[:, z]
                    gain_c[8 * block + kk, half] = square[:, z]

    def first_depth():
        for i in range(5, len(loads)):
            loads[i].wait()
        depth_term(0)

    def first_lap():
        @pl.loop(0, N // 2)
        def _(pair):
            for u in range(2):
                for half in range(2):
                    lap[2 * pair + u, half] = laplace(0, 2 * pair + u, half)

        await_halos(0)
        for side in range(2):
            for half in range(2):
                for i, value in enumerate(corrections(unpack_layers(x_in.at[0, side], side, half), side)):
                    lap[28 * side + i, half] = lap[28 * side + i, half] + value
        y_corrections(0)

        @pl.loop(0, N)
        def _(x):
            for half in range(2):
                for side in range(2):
                    rows = slice(28 * side, 28 * side + 4)
                    lap[x, half, rows, :] = lap[x, half, rows, :] + corner[side, half, pl.ds(x, 4, stride=N), :]

    forward(0)
    forward(1)
    first_depth()
    forward(2)
    select(0)
    forward(3)
    forward(4)
    select(1)
    first_lap()
    gains(0)
    select(2)
    gains(1)
    select(3)
    select(4)
    gains(2)
    gains(3)
    gains(4)

    def step(t):
        before_p = p_m if t == 0 else p[t - 1]
        before_q = q_m if t == 0 else q[t - 1]
        off = 0 if t == 0 else 4
        y0 = 0 if t == 0 else 8
        last = t == STEPS - 1

        def plane(x):
            k = lax.rem(x + shift, N)
            amount = jnp.where(x + gx * N == sources[0, 0], wavelet[0, t], jnp.float32(0))
            for half in range(2):
                h = lap[x, half] if t == 0 else laplace(t, x, half)
                z = deep[x, half]
                a, b, c = gain_a[k, half], gain_b[k, half], gain_c[k, half]
                new_p = (2.0 * p[t][x + 4, half, 8:40, :] - before_p[x + off, half, y0:y0 + N, :]) + (a * h + b * z)
                new_p = new_p + amount * spot[half]
                new_q = (2.0 * q[t][x, half] - before_q[x, half]) + (b * h + c * z)
                if last:
                    p_out[0, x, :, 128 * half:128 * half + 128] = new_p
                    q_out[0, x, :, 128 * half:128 * half + 128] = new_q
                else:
                    q[t + 1][x, half] = new_q
                    p[t + 1][x + 4, half, 8:40, :] = new_p
                    if t == 0:
                        stage[0, half, pl.ds(x, 4, stride=N), :] = new_p[0:4]
                        stage[1, half, pl.ds(x, 4, stride=N), :] = new_p[28:32]

        @pl.loop(0, N // 2)
        def _(pair):
            plane(2 * pair)
            plane(2 * pair + 1)

    def add_rims(t):
        last = t == STEPS - 1

        def bump(x, k, half, first, count, value):
            rows = slice(first, first + count)
            add_p = gain_a[k, half, rows, :] * value
            add_q = gain_b[k, half, rows, :] * value
            if last:
                z = slice(128 * half, 128 * half + 128)
                p_out[0, x, rows, z] = p_out[0, x, rows, z] + add_p
                q_out[0, x, rows, z] = q_out[0, x, rows, z] + add_q
                return None
            lower = slice(8 + first, 8 + first + count)
            new_p = p[t + 1][x + 4, half, lower, :] + add_p
            p[t + 1][x + 4, half, lower, :] = new_p
            q[t + 1][x, half, rows, :] = q[t + 1][x, half, rows, :] + add_q
            return new_p

        await_halos(t)
        for side in range(2):
            for half in range(2):
                for i, value in enumerate(corrections(unpack_layers(x_in.at[t, side], side, half), side)):
                    x = 28 * side + i
                    bump(x, lax.rem(x + shift, N), half, 0, N, value)
        y_corrections(t)

        @pl.loop(0, N // 2)
        def _(pair):
            for u in range(2):
                x = 2 * pair + u
                k = lax.rem(x + shift, N)
                for half in range(2):
                    for side in range(2):
                        new_p = bump(x, k, half, 28 * side, 4, corner[side, half, pl.ds(x, 4, stride=N), :])
                        if not last:
                            stage[side, half, pl.ds(x, 4, stride=N), :] = new_p

    for t in range(STEPS):
        if t > 0:
            depth_term(t)
        step(t)
        if t > 0:
            add_rims(t)
        if t < STEPS - 1:
            send_rims(t + 1)

    for c in range(CHUNKS):
        for d in range(3):
            spread[c, d].wait_send()
            deal[c, d].wait_send()
        for d in range(4):
            x_copy[c, d].wait_send()
        core_copy[c, 0].wait_send()
        core_copy[c, 1].wait_send()


def on_device(velocity, epsilon, delta, anchors, sources, wavelet, p_now, p_prev, q_now, q_prev):
    out = pltpu.VMEM(p_now.shape, jnp.float32)
    vmem = pl.BlockSpec(memory_space=pltpu.VMEM)
    hbm = pl.BlockSpec(memory_space=pl.ANY)
    smem = pl.BlockSpec(memory_space=pltpu.SMEM)
    f32 = jnp.float32
    bf16 = jnp.bfloat16
    block = pltpu.VMEM((N, 2, N, 128), f32)
    padded = pltpu.VMEM((N + 8, 2, N + 16, 128), f32)
    rims = pltpu.VMEM((STEPS, 2, 5, 2, N, 128), bf16)
    dma = pltpu.SemaphoreType.DMA
    return pl.pallas_call(
        kernel,
        out_shape=(out, out),
        in_specs=[hbm, hbm, hbm, smem, smem, smem, hbm, hbm, hbm, hbm],
        out_specs=(vmem, vmem),
        scratch_shapes=[
            pltpu.VMEM((3, N, N, 256), bf16),
            *[pltpu.VMEM((4, 4, 3, rows, N, 256), bf16) for rows in ROWS],
            pltpu.VMEM((3, 3, 8, N, 256), bf16),
            pltpu.VMEM((3, 4, 8, N, 256), bf16),
            block, block, block, block, block,
            pltpu.VMEM((256, 256), bf16), pltpu.VMEM((256, 256), bf16), pltpu.VMEM((2, N, 128), f32),
            block, padded, padded, padded, padded,
            block, block, block, block, block,
            pltpu.VMEM((2, 2, 4 * N, 128), f32), pltpu.VMEM((2, 2, 4 * N, 128), f32),
            rims, rims, rims, rims,
            dma((11,)), dma((CHUNKS, 3)), dma((CHUNKS, 3)), dma((CHUNKS,)), dma((CHUNKS, 4)), dma((CHUNKS, 4)),
            dma((CHUNKS, 2)), dma((CHUNKS, 2)), dma((CHUNKS, 3)), dma((CHUNKS, 3)),
            dma((STEPS, 4)), dma((STEPS, 4)),
        ],
        compiler_params=pltpu.CompilerParams(
            collective_id=0, has_side_effects=True, vmem_limit_bytes=56 << 20),
        name="migrate",
    )(velocity, epsilon, delta, anchors, sources, wavelet, p_now, p_prev, q_now, q_prev)


def solution(mesh):
    field = P("shot", "gx", "gy", None)
    model = P(("shot", "gx"), "gy", None)
    return jax.shard_map(
        on_device,
        mesh=mesh,
        in_specs=(model, model, model, P(), P("shot", None), P("shot", None), field, field, field, field),
        out_specs=(field, field),
        check_vma=False,
    )
```

```python
import jax
import jax.numpy as jnp
from jax import lax
from jax.experimental import pallas as pl
from jax.experimental.pallas import tpu as pltpu
from jax.sharding import PartitionSpec as P

STEPS = 4
WEIGHTS = (-205.0 / 72.0, 8.0 / 5.0, -1.0 / 5.0, 8.0 / 315.0, -1.0 / 560.0)
MESH = pl.DeviceIdType.MESH
N = 32
PIECES = ((0, 0, 32), (1, 0, 32), (2, 0, 32), (3, 0, 16), (3, 16, 16))
CHUNKS = len(PIECES)
HOPS = (1, 3, 2)
PARTNERS = ((0, 1), (1, 1), (0, 3), (1, 3), (0, 2), (1, 2), (1, 0))


def kernel(
    velocity, epsilon, delta, anchors, sources, wavelet, p_now, p_prev, q_now, q_prev,
    p_out, q_out,
    slab, *scratch,
):
    gathered = scratch[:CHUNKS]
    (outgoing, window,
    gain_a, gain_b, gain_c, lap, deep, band_hi, band_lo, spot,
    p_m, p_0, p_1, p_2, p_3, q_m, q_0, q_1, q_2, q_3,
    stage, corner, x_out, x_in, y_out, y_in,
    load_sem, spread_send, spread_recv, own_sem, x_send, x_recv,
    deal_send, deal_recv, halo_send, halo_recv) = scratch[CHUNKS:]
    p = (p_0, p_1, p_2, p_3)
    q = (q_0, q_1, q_2, q_3)
    shot = lax.axis_index("shot")
    gx = lax.axis_index("gx")
    gy = lax.axis_index("gy")
    far = lax.rem(shot + 2, 4)
    mate = shot + 1 - 2 * lax.rem(shot, 2)
    core = lax.rem(shot, 2)
    pair = shot - core
    shots = (shot, mate)
    first_row = (4 * core, 4 - 4 * core)
    has_gx = (gx > 0, gx < 3)
    has_gy = (gy > 0, gy < 7)

    def to(s, z, y):
        return (s, z, y)

    barrier = pltpu.get_barrier_semaphore()
    for hop in HOPS:
        pl.semaphore_signal(barrier, inc=1, device_id=to(shot, lax.rem(gx + hop, 4), gy), device_id_type=MESH)
    pl.semaphore_signal(barrier, inc=1, device_id=to(far, gx, gy), device_id_type=MESH)
    for hop in range(4):
        pl.semaphore_signal(barrier, inc=1, device_id=to(mate, lax.rem(gx + hop, 4), gy), device_id_type=MESH)
    for side in range(2):
        @pl.when(has_gy[side])
        def _():
            pl.semaphore_signal(barrier, inc=1, device_id=to(shot, gx, gy + 2 * side - 1), device_id_type=MESH)

    loads = []
    def load(src, dst):
        copy = pltpu.make_async_copy(src, dst, load_sem.at[len(loads)])
        copy.start()
        loads.append(copy)
    for m, model in enumerate((velocity, epsilon, delta)):
        load(model, slab.at[m])
    for half in range(2):
        z = pl.ds(128 * half, 128)
        load(p_now.at[0, :, :, z], p_0.at[pl.ds(4, N), half, pl.ds(8, N), :])
    for src, dst in ((p_prev, p_m), (q_now, q_0), (q_prev, q_m)):
        for half in range(2):
            load(src.at[0, :, :, pl.ds(128 * half, 128)], dst.at[:, half])

    pl.semaphore_wait(barrier, 8 + has_gy[0].astype(jnp.int32) + has_gy[1].astype(jnp.int32))

    for m in range(3):
        loads[m].wait()
    spread = {}
    x_copy = {}
    def scatter(c):
        for other, hop in PARTNERS:
            z = lax.rem(gx + hop, 4)
            spread[c, other, hop] = pltpu.make_async_remote_copy(
                src_ref=slab.at[:, 8 * z + first_row[other] + PIECES[c][0], pl.ds(PIECES[c][1], PIECES[c][2])],
                dst_ref=gathered[c].at[shot, gx],
                send_sem=spread_send.at[c, other, hop], recv_sem=spread_recv.at[c, other, hop],
                device_id=to(shots[other], z, gy), device_id_type=MESH)
            spread[c, other, hop].start()

    def cross(c, piece, src, dst):
        x_copy[c, piece] = pltpu.make_async_remote_copy(
            src_ref=src, dst_ref=dst, send_sem=x_send.at[c, piece], recv_sem=x_recv.at[c, piece],
            device_id=to(far, gx, gy), device_id_type=MESH)
        x_copy[c, piece].start()

    def own_rows(c):
        return slab.at[:, 8 * gx + first_row[0] + PIECES[c][0], pl.ds(PIECES[c][1], PIECES[c][2])]

    for c in range(CHUNKS):
        scatter(c)
        cross(c, 0, own_rows(c), gathered[c].at[shot, gx])
    own = []
    for c in range(CHUNKS):
        own.append(pltpu.make_async_copy(own_rows(c), gathered[c].at[shot, gx], own_sem.at[c]))
        own[c].start()

    def x_halo(t, side):
        return pltpu.make_async_remote_copy(
            src_ref=x_out.at[t, side], dst_ref=x_in.at[t, 1 - side],
            send_sem=halo_send.at[t, side], recv_sem=halo_recv.at[t, side],
            device_id=to(shot, gx + 2 * side - 1, gy), device_id_type=MESH)

    def y_halo(t, side):
        return pltpu.make_async_remote_copy(
            src_ref=y_out.at[t, side], dst_ref=y_in.at[t, 1 - side],
            send_sem=halo_send.at[t, 2 + side], recv_sem=halo_recv.at[t, 2 + side],
            device_id=to(shot, gx, gy + 2 * side - 1), device_id_type=MESH)

    def pack_layers(out, side, layer, half, values):
        near = 3 if side else 0
        hi = values.astype(jnp.bfloat16)
        out[layer, half] = hi
        if layer == near:
            out[4, half] = (values - hi.astype(jnp.float32)).astype(jnp.bfloat16)

    def unpack_layers(source, side, half):
        near = 0 if side else 3
        layers = [source[layer, half].astype(jnp.float32) for layer in range(4)]
        layers[near] = layers[near] + source[4, half].astype(jnp.float32)
        return layers

    def corrections(layers, side):
        result = []
        for i in range(4):
            reach = range(i + 1) if side else range(i, 4)
            terms = [WEIGHTS[4 + j - i if side else i + 4 - j] * layers[j] for j in reach]
            total = terms[0]
            for term in terms[1:]:
                total = total + term
            result.append(total)
        return result

    def send_y(t):
        for side in range(2):
            for half in range(2):
                for layer in range(4):
                    pack_layers(y_out.at[t, side], side, layer, half, stage[side, half, N * layer:N * layer + N, :])
            @pl.when(has_gy[side])
            def _():
                y_halo(t, side).start()

    def send_x(t):
        for side in range(2):
            for half in range(2):
                for layer in range(4):
                    pack_layers(x_out.at[t, side], side, layer, half, p[t][4 + 28 * side + layer, half, 8:40, :])
            @pl.when(has_gx[side])
            def _():
                x_halo(t, side).start()

    def send_rims(t):
        send_y(t)
        send_x(t)

    def await_x(t):
        for side in range(2):
            @pl.when(has_gx[side])
            def _():
                x_halo(t, 1 - side).wait_recv()

    def await_y(t):
        for side in range(2):
            @pl.when(has_gy[side])
            def _():
                y_halo(t, 1 - side).wait_recv()

    def y_corrections(t):
        for side in range(2):
            for half in range(2):
                for i, value in enumerate(corrections(unpack_layers(y_in.at[t, side], side, half), side)):
                    corner[side, half, N * i:N * i + N, :] = value

    for side in range(2):
        @pl.when(jnp.logical_not(has_gx[side]))
        def _():
            for t in range(STEPS):
                x_in[t, side] = jnp.zeros((5, 2, N, 128), jnp.bfloat16)

        @pl.when(jnp.logical_not(has_gy[side]))
        def _():
            for t in range(STEPS):
                y_in[t, side] = jnp.zeros((5, 2, N, 128), jnp.bfloat16)

    for t in range(STEPS):
        @pl.loop(0, 4)
        def _(x):
            for half in range(2):
                p[t][x, half, 8:40, :] = jnp.zeros((N, 128), jnp.float32)
                p[t][x + 36, half, 8:40, :] = jnp.zeros((N, 128), jnp.float32)

        @pl.loop(0, N)
        def _(x):
            for half in range(2):
                p[t][x + 4, half, 0:8, :] = jnp.zeros((8, 128), jnp.float32)
                p[t][x + 4, half, 40:48, :] = jnp.zeros((8, 128), jnp.float32)

    row = lax.broadcasted_iota(jnp.int32, (256, 256), 0)
    col = lax.broadcasted_iota(jnp.int32, (256, 256), 1)
    apart = jnp.abs(row - col)
    band = jnp.zeros((256, 256), jnp.float32)
    for k in range(5):
        band = jnp.where(apart == k, jnp.float32(WEIGHTS[k]), band)
    hi = band.astype(jnp.bfloat16)
    band_hi[...] = hi
    band_lo[...] = (band - hi.astype(jnp.float32)).astype(jnp.bfloat16)
    y_at = lax.broadcasted_iota(jnp.int32, (N, 128), 0) + gy * N
    z_at = lax.broadcasted_iota(jnp.int32, (N, 128), 1)
    for half in range(2):
        here = jnp.logical_and(y_at == sources[0, 1], z_at + 128 * half == sources[0, 2])
        spot[half] = jnp.where(here, jnp.float32(1), jnp.float32(0))

    for i in range(3, 5):
        loads[i].wait()

    @pl.loop(0, N)
    def _(x):
        for half in range(2):
            stage[0, half, pl.ds(x, 4, stride=N), :] = p_0[x + 4, half, 8:12, :]
            stage[1, half, pl.ds(x, 4, stride=N), :] = p_0[x + 4, half, 36:40, :]
    send_rims(0)

    def forward(c):
        spread[c, 1, 0].wait_recv()
        cross(c, 1, gathered[c].at[mate, gx], gathered[c].at[mate, gx])
        for d, hop in enumerate(HOPS):
            spread[c, 0, hop].wait_recv()
            spread[c, 1, hop].wait_recv()
            z = lax.rem(gx + 4 - hop, 4)
            both = gathered[c].at[pl.ds(pair, 2), z]
            cross(c, d + 2, both, both)
        own[c].wait()

    def depth_term(t):
        values = jnp.concatenate([q[t][:, 0].reshape(N * N, 128), q[t][:, 1].reshape(N * N, 128)], axis=-1)
        hi = values.astype(jnp.bfloat16)
        lo = (values - hi.astype(jnp.float32)).astype(jnp.bfloat16)
        total = jnp.dot(hi, band_hi[...], preferred_element_type=jnp.float32)
        total = total + jnp.dot(lo, band_hi[...], preferred_element_type=jnp.float32)
        total = total + jnp.dot(hi, band_lo[...], preferred_element_type=jnp.float32)
        deep[:, 0] = total[:, :128].reshape(N, N, 128)
        deep[:, 1] = total[:, 128:].reshape(N, N, 128)

    def laplace(t, x, half):
        total = (2.0 * WEIGHTS[0]) * p[t][x + 4, half, 8:40, :]
        for k in range(1, 5):
            pair = p[t][x + 4 + k, half, 8:40, :] + p[t][x + 4 - k, half, 8:40, :]
            pair = pair + (p[t][x + 4, half, 8 + k:40 + k, :] + p[t][x + 4, half, 8 - k:40 - k, :])
            total = total + WEIGHTS[k] * pair
        return total

    bases = [lax.div(anchors[g], N) for g in shots]
    shifts = [lax.rem(anchors[g], N) for g in shots]
    shift = shifts[0]
    deal = {}

    def select(c):
        for piece in range(5):
            x_copy[c, piece].wait_recv()
        for slot, (other, hop) in enumerate(PARTNERS + ((0, 0),)):
            z = lax.rem(gx + hop, 4)
            mine = (other, hop) == (0, 0)
            row = first_row[0] + PIECES[c][0]
            cells = pl.ds(PIECES[c][1], PIECES[c][2])
            at = jnp.minimum(bases[other] + z + (8 * gx + row < shifts[other]).astype(jnp.int32), 15)
            values = gathered[c][lax.div(at, 4), lax.rem(at, 4)]
            if mine:
                window[:, gx, row, cells] = values
            else:
                outgoing[slot, :, PIECES[c][0], cells] = values
                deal[c, slot] = pltpu.make_async_remote_copy(
                    src_ref=outgoing.at[slot, :, PIECES[c][0], cells],
                    dst_ref=window.at[:, gx, row, cells],
                    send_sem=deal_send.at[c, slot], recv_sem=deal_recv.at[c, slot],
                    device_id=to(shots[other], z, gy), device_id_type=MESH)
                deal[c, slot].start()

    def gains(c):
        for slot in range(7):
            deal[c, slot].wait_recv()

        @pl.loop(0, 8)
        def _(block):
            kk, y0, count = PIECES[c]
            cells = slice(y0, y0 + count)
            row = 4 * lax.rem(block, 2) + kk
            speed = window[0, lax.div(block, 2), row, cells].astype(jnp.float32)
            eps = window[1, lax.div(block, 2), row, cells].astype(jnp.float32)
            dlt = window[2, lax.div(block, 2), row, cells].astype(jnp.float32)
            square = speed * speed
            cross_term = square * jnp.sqrt(1.0 + 2.0 * dlt)
            horiz = square * (1.0 + 2.0 * eps)
            for half in range(2):
                z = slice(128 * half, 128 * half + 128)
                gain_a[4 * block + kk, half, cells] = horiz[:, z]
                gain_b[4 * block + kk, half, cells] = cross_term[:, z]
                gain_c[4 * block + kk, half, cells] = square[:, z]

    def first_depth():
        for i in range(5, len(loads)):
            loads[i].wait()
        depth_term(0)

    def first_lap():
        @pl.loop(0, N // 2)
        def _(pair):
            for u in range(2):
                for half in range(2):
                    lap[2 * pair + u, half] = laplace(0, 2 * pair + u, half)

        await_x(0)
        await_y(0)
        for side in range(2):
            for half in range(2):
                for i, value in enumerate(corrections(unpack_layers(x_in.at[0, side], side, half), side)):
                    lap[28 * side + i, half] = lap[28 * side + i, half] + value
        y_corrections(0)

        @pl.loop(0, N)
        def _(x):
            for half in range(2):
                for side in range(2):
                    rows = slice(28 * side, 28 * side + 4)
                    lap[x, half, rows, :] = lap[x, half, rows, :] + corner[side, half, pl.ds(x, 4, stride=N), :]

    forward(0)
    forward(1)
    first_depth()
    forward(2)
    select(0)
    forward(3)
    forward(4)
    select(1)
    first_lap()
    gains(0)
    select(2)
    gains(1)
    select(3)
    select(4)
    gains(2)
    gains(3)
    gains(4)

    def step(t, do_p, do_q):
        before_p = p_m if t == 0 else p[t - 1]
        before_q = q_m if t == 0 else q[t - 1]
        off = 0 if t == 0 else 4
        y0 = 0 if t == 0 else 8
        last = t == STEPS - 1

        def plane(x):
            k = lax.rem(x + shift, N)
            amount = jnp.where(x + gx * N == sources[0, 0], wavelet[0, t], jnp.float32(0))
            for half in range(2):
                h = lap[x, half] if t == 0 else laplace(t, x, half)
                z = deep[x, half]
                b = gain_b[k, half]
                if do_p:
                    new_p = (2.0 * p[t][x + 4, half, 8:40, :] - before_p[x + off, half, y0:y0 + N, :]) + (
                        gain_a[k, half] * h + b * z)
                    new_p = new_p + amount * spot[half]
                    if last:
                        p_out[0, x, :, 128 * half:128 * half + 128] = new_p
                    else:
                        p[t + 1][x + 4, half, 8:40, :] = new_p
                    if t == 0:
                        stage[0, half, pl.ds(x, 4, stride=N), :] = new_p[0:4]
                        stage[1, half, pl.ds(x, 4, stride=N), :] = new_p[28:32]
                if do_q:
                    new_q = (2.0 * q[t][x, half] - before_q[x, half]) + (b * h + gain_c[k, half] * z)
                    if last:
                        q_out[0, x, :, 128 * half:128 * half + 128] = new_q
                    else:
                        q[t + 1][x, half] = new_q

        @pl.loop(0, N // 2)
        def _(pair):
            plane(2 * pair)
            plane(2 * pair + 1)

    def bump_p(t, x, k, half, first, count, value):
        rows = slice(first, first + count)
        add = gain_a[k, half, rows, :] * value
        if t == STEPS - 1:
            z = slice(128 * half, 128 * half + 128)
            p_out[0, x, rows, z] = p_out[0, x, rows, z] + add
        else:
            lower = slice(8 + first, 8 + first + count)
            new_p = p[t + 1][x + 4, half, lower, :] + add
            p[t + 1][x + 4, half, lower, :] = new_p
            if count == 4:
                stage[first // 28, half, pl.ds(x, 4, stride=N), :] = new_p

    def bump_q(t, x, k, half, first, count, value):
        rows = slice(first, first + count)
        add = gain_b[k, half, rows, :] * value
        if t == STEPS - 1:
            z = slice(128 * half, 128 * half + 128)
            q_out[0, x, rows, z] = q_out[0, x, rows, z] + add
        else:
            q[t + 1][x, half, rows, :] = q[t + 1][x, half, rows, :] + add

    def add_x(t, bumps):
        for side in range(2):
            for half in range(2):
                for i, value in enumerate(corrections(unpack_layers(x_in.at[t, side], side, half), side)):
                    x = 28 * side + i
                    for bump in bumps:
                        bump(t, x, lax.rem(x + shift, N), half, 0, N, value)

    def add_y(t, bumps):
        @pl.loop(0, N // 2)
        def _(pair):
            for u in range(2):
                x = 2 * pair + u
                k = lax.rem(x + shift, N)
                for half in range(2):
                    for side in range(2):
                        value = corner[side, half, pl.ds(x, 4, stride=N), :]
                        for bump in bumps:
                            bump(t, x, k, half, 28 * side, 4, value)

    step(0, True, False)
    send_rims(1)
    step(0, False, True)
    for t in range(1, STEPS):
        depth_term(t)
        step(t, True, True)
        await_x(t)
        add_x(t, (bump_p, bump_q))
        await_y(t)
        y_corrections(t)
        if t < STEPS - 1:
            add_y(t, (bump_p,))
            send_rims(t + 1)
            add_y(t, (bump_q,))
        else:
            add_y(t, (bump_p, bump_q))

    for side in range(2):
        @pl.when(has_gx[side])
        def _():
            for t in range(STEPS):
                x_halo(t, side).wait_send()

        @pl.when(has_gy[side])
        def _():
            for t in range(STEPS):
                y_halo(t, side).wait_send()

    for c in range(CHUNKS):
        for slot, (other, hop) in enumerate(PARTNERS):
            spread[c, other, hop].wait_send()
            deal[c, slot].wait_send()
        for piece in range(5):
            x_copy[c, piece].wait_send()


def keep(p_in, q_in, p_out, q_out, sem):
    copies = [pltpu.make_async_copy(p_in, p_out, sem.at[0]), pltpu.make_async_copy(q_in, q_out, sem.at[1])]
    for copy in copies:
        copy.start()
    for copy in copies:
        copy.wait()


def on_device(velocity, epsilon, delta, anchors, sources, wavelet, p_now, p_prev, q_now, q_prev):
    out = pltpu.VMEM(p_now.shape, jnp.float32)
    vmem = pl.BlockSpec(memory_space=pltpu.VMEM)
    hbm = pl.BlockSpec(memory_space=pl.ANY)
    smem = pl.BlockSpec(memory_space=pltpu.SMEM)
    f32 = jnp.float32
    bf16 = jnp.bfloat16
    block = pltpu.VMEM((N, 2, N, 128), f32)
    padded = pltpu.VMEM((N + 8, 2, N + 16, 128), f32)
    rims = pltpu.VMEM((STEPS, 2, 5, 2, N, 128), bf16)
    dma = pltpu.SemaphoreType.DMA
    p_end, q_end = pl.pallas_call(
        kernel,
        out_shape=(out, out),
        in_specs=[hbm, hbm, hbm, smem, smem, smem, hbm, hbm, hbm, hbm],
        out_specs=(vmem, vmem),
        scratch_shapes=[
            pltpu.VMEM((3, N, N, 256), bf16),
            *[pltpu.VMEM((4, 4, 3, count, 256), bf16) for _, _, count in PIECES],
            pltpu.VMEM((7, 3, 4, N, 256), bf16),
            pltpu.VMEM((3, 4, 8, N, 256), bf16),
            block, block, block, block, block,
            pltpu.VMEM((256, 256), bf16), pltpu.VMEM((256, 256), bf16), pltpu.VMEM((2, N, 128), f32),
            block, padded, padded, padded, padded,
            block, block, block, block, block,
            pltpu.VMEM((2, 2, 4 * N, 128), f32), pltpu.VMEM((2, 2, 4 * N, 128), f32),
            rims, rims, rims, rims,
            dma((11,)), dma((CHUNKS, 2, 4)), dma((CHUNKS, 2, 4)), dma((CHUNKS,)), dma((CHUNKS, 5)), dma((CHUNKS, 5)),
            dma((CHUNKS, 7)), dma((CHUNKS, 7)),
            dma((STEPS, 4)), dma((STEPS, 4)),
        ],
        compiler_params=pltpu.CompilerParams(
            collective_id=0, has_side_effects=True, vmem_limit_bytes=56 << 20),
        name="migrate",
    )(velocity, epsilon, delta, anchors, sources, wavelet, p_now, p_prev, q_now, q_prev)
    result = jax.ShapeDtypeStruct(p_now.shape, f32)
    return pl.pallas_call(
        keep,
        out_shape=(result, result),
        in_specs=[vmem, vmem],
        out_specs=(hbm, hbm),
        scratch_shapes=[dma((2,))],
        name="keep",
    )(pltpu.with_memory_space_constraint(p_end, pltpu.VMEM), pltpu.with_memory_space_constraint(q_end, pltpu.VMEM))


def solution(mesh):
    field = P("shot", "gx", "gy", None)
    model = P(("shot", "gx"), "gy", None)
    return jax.shard_map(
        on_device,
        mesh=mesh,
        in_specs=(model, model, model, P(), P("shot", None), P("shot", None), field, field, field, field),
        out_specs=(field, field),
        check_vma=False,
    )
```

```python
import jax
import jax.numpy as jnp
from jax import lax
from jax.experimental import pallas as pl
from jax.experimental.pallas import tpu as pltpu
from jax.sharding import PartitionSpec as P

STEPS = 4
WEIGHTS = (-205.0 / 72.0, 8.0 / 5.0, -1.0 / 5.0, 8.0 / 315.0, -1.0 / 560.0)
MESH = pl.DeviceIdType.MESH
N = 32
PIECES = ((0, 0, 32), (1, 0, 32), (2, 0, 32), (3, 0, 16), (3, 16, 16))
CHUNKS = len(PIECES)
HOPS = (1, 3, 2)
PARTNERS = ((0, 1), (1, 1), (0, 3), (1, 3), (0, 2), (1, 2), (1, 0))


def kernel(
    velocity, epsilon, delta, anchors, sources, wavelet, p_now, p_prev, q_now, q_prev,
    p_out, q_out,
    slab, *scratch,
):
    gathered = scratch[:CHUNKS]
    (outgoing, window,
    gain_a, gain_b, gain_c, lap, deep, band_hi, band_lo, spot,
    p_m, p_0, p_1, p_2, p_3, q_m, q_0, q_1, q_2, q_3,
    stage, corner, face, x_out, x_in, y_out, y_in,
    load_sem, spread_send, spread_recv, own_sem, x_send, x_recv,
    deal_send, deal_recv, halo_send, halo_recv) = scratch[CHUNKS:]
    p = (p_0, p_1, p_2, p_3)
    q = (q_0, q_1, q_2, q_3)
    shot = lax.axis_index("shot")
    gx = lax.axis_index("gx")
    gy = lax.axis_index("gy")
    far = lax.rem(shot + 2, 4)
    mate = shot + 1 - 2 * lax.rem(shot, 2)
    core = lax.rem(shot, 2)
    pair = shot - core
    shots = (shot, mate)
    first_row = (4 * core, 4 - 4 * core)
    has_gx = (gx > 0, gx < 3)
    has_gy = (gy > 0, gy < 7)

    def to(s, z, y):
        return (s, z, y)

    barrier = pltpu.get_barrier_semaphore()
    for hop in HOPS:
        pl.semaphore_signal(barrier, inc=1, device_id=to(shot, lax.rem(gx + hop, 4), gy), device_id_type=MESH)
    pl.semaphore_signal(barrier, inc=1, device_id=to(far, gx, gy), device_id_type=MESH)
    for hop in range(4):
        pl.semaphore_signal(barrier, inc=1, device_id=to(mate, lax.rem(gx + hop, 4), gy), device_id_type=MESH)
    for side in range(2):
        @pl.when(has_gy[side])
        def _():
            pl.semaphore_signal(barrier, inc=1, device_id=to(shot, gx, gy + 2 * side - 1), device_id_type=MESH)

    loads = []
    def load(src, dst):
        copy = pltpu.make_async_copy(src, dst, load_sem.at[len(loads)])
        copy.start()
        loads.append(copy)
    for m, model in enumerate((velocity, epsilon, delta)):
        load(model, slab.at[m])
    for half in range(2):
        z = pl.ds(128 * half, 128)
        load(p_now.at[0, :, :, z], p_0.at[pl.ds(4, N), half, pl.ds(8, N), :])
    for src, dst in ((p_prev, p_m), (q_now, q_0), (q_prev, q_m)):
        for half in range(2):
            load(src.at[0, :, :, pl.ds(128 * half, 128)], dst.at[:, half])

    pl.semaphore_wait(barrier, 8 + has_gy[0].astype(jnp.int32) + has_gy[1].astype(jnp.int32))

    for m in range(3):
        loads[m].wait()
    spread = {}
    x_copy = {}
    def scatter(c):
        for other, hop in PARTNERS:
            z = lax.rem(gx + hop, 4)
            spread[c, other, hop] = pltpu.make_async_remote_copy(
                src_ref=slab.at[:, 8 * z + first_row[other] + PIECES[c][0], pl.ds(PIECES[c][1], PIECES[c][2])],
                dst_ref=gathered[c].at[shot, gx],
                send_sem=spread_send.at[c, other, hop], recv_sem=spread_recv.at[c, other, hop],
                device_id=to(shots[other], z, gy), device_id_type=MESH)
            spread[c, other, hop].start()

    def cross(c, piece, src, dst):
        x_copy[c, piece] = pltpu.make_async_remote_copy(
            src_ref=src, dst_ref=dst, send_sem=x_send.at[c, piece], recv_sem=x_recv.at[c, piece],
            device_id=to(far, gx, gy), device_id_type=MESH)
        x_copy[c, piece].start()

    def own_rows(c):
        return slab.at[:, 8 * gx + first_row[0] + PIECES[c][0], pl.ds(PIECES[c][1], PIECES[c][2])]

    for c in range(CHUNKS):
        cross(c, 0, own_rows(c), gathered[c].at[shot, gx])
    for c in range(CHUNKS):
        scatter(c)
    own = []
    for c in range(CHUNKS):
        own.append(pltpu.make_async_copy(own_rows(c), gathered[c].at[shot, gx], own_sem.at[c]))
        own[c].start()

    def x_halo(t, side):
        return pltpu.make_async_remote_copy(
            src_ref=x_out.at[t, side], dst_ref=x_in.at[t, 1 - side],
            send_sem=halo_send.at[t, side], recv_sem=halo_recv.at[t, side],
            device_id=to(shot, gx + 2 * side - 1, gy), device_id_type=MESH)

    def y_halo(t, side, half):
        return pltpu.make_async_remote_copy(
            src_ref=y_out.at[t, side, half], dst_ref=y_in.at[t, 1 - side, half],
            send_sem=halo_send.at[t, 2 + 2 * side + half], recv_sem=halo_recv.at[t, 2 + 2 * side + half],
            device_id=to(shot, gx, gy + 2 * side - 1), device_id_type=MESH)

    def pack_layers(out, side, layer, values):
        near = 3 if side else 0
        hi = values.astype(jnp.bfloat16)
        out[layer] = hi
        if layer == near:
            out[4] = (values - hi.astype(jnp.float32)).astype(jnp.bfloat16)

    def unpack_layers(source, side):
        near = 0 if side else 3
        layers = [source[layer].astype(jnp.float32) for layer in range(4)]
        layers[near] = layers[near] + source[4].astype(jnp.float32)
        return layers

    def corrections(layers, side):
        result = []
        for i in range(4):
            reach = range(i + 1) if side else range(i, 4)
            terms = [WEIGHTS[4 + j - i if side else i + 4 - j] * layers[j] for j in reach]
            total = terms[0]
            for term in terms[1:]:
                total = total + term
            result.append(total)
        return result

    def send_y(t, half):
        for side in range(2):
            for layer in range(4):
                pack_layers(y_out.at[t, side, half], side, layer, stage[side, half, N * layer:N * layer + N, :])

            @pl.when(has_gy[side])
            def _():
                y_halo(t, side, half).start()

    def send_x(t):
        for side in range(2):
            for half in range(2):
                for layer in range(4):
                    pack_layers(x_out.at[t, side, half], side, layer, p[t][4 + 28 * side + layer, half, 8:40, :])
            @pl.when(has_gx[side])
            def _():
                x_halo(t, side).start()

    def send_rims(t):
        send_y(t, 0)
        send_y(t, 1)
        send_x(t)

    def await_x(t):
        for side in range(2):
            @pl.when(has_gx[side])
            def _():
                x_halo(t, 1 - side).wait_recv()

    def await_y(t, half):
        for side in range(2):
            @pl.when(has_gy[side])
            def _():
                y_halo(t, 1 - side, half).wait_recv()
        for side in range(2):
            for i, value in enumerate(corrections(unpack_layers(y_in.at[t, side, half], side), side)):
                corner[side, half, N * i:N * i + N, :] = value

    for side in range(2):
        @pl.when(jnp.logical_not(has_gx[side]))
        def _():
            for t in range(STEPS):
                x_in[t, side] = jnp.zeros((2, 5, N, 128), jnp.bfloat16)

        @pl.when(jnp.logical_not(has_gy[side]))
        def _():
            for t in range(STEPS):
                y_in[t, side] = jnp.zeros((2, 5, N, 128), jnp.bfloat16)

    for t in range(STEPS):
        @pl.loop(0, 4)
        def _(x):
            for half in range(2):
                p[t][x, half, 8:40, :] = jnp.zeros((N, 128), jnp.float32)
                p[t][x + 36, half, 8:40, :] = jnp.zeros((N, 128), jnp.float32)

        @pl.loop(0, N)
        def _(x):
            for half in range(2):
                p[t][x + 4, half, 0:8, :] = jnp.zeros((8, 128), jnp.float32)
                p[t][x + 4, half, 40:48, :] = jnp.zeros((8, 128), jnp.float32)

    row = lax.broadcasted_iota(jnp.int32, (256, 256), 0)
    col = lax.broadcasted_iota(jnp.int32, (256, 256), 1)
    apart = jnp.abs(row - col)
    band = jnp.zeros((256, 256), jnp.float32)
    for k in range(5):
        band = jnp.where(apart == k, jnp.float32(WEIGHTS[k]), band)
    hi = band.astype(jnp.bfloat16)
    band_hi[...] = hi
    band_lo[...] = (band - hi.astype(jnp.float32)).astype(jnp.bfloat16)
    y_at = lax.broadcasted_iota(jnp.int32, (N, 128), 0) + gy * N
    z_at = lax.broadcasted_iota(jnp.int32, (N, 128), 1)
    for half in range(2):
        here = jnp.logical_and(y_at == sources[0, 1], z_at + 128 * half == sources[0, 2])
        spot[half] = jnp.where(here, jnp.float32(1), jnp.float32(0))

    for i in range(3, 5):
        loads[i].wait()

    @pl.loop(0, N)
    def _(x):
        for half in range(2):
            stage[0, half, pl.ds(x, 4, stride=N), :] = p_0[x + 4, half, 8:12, :]
            stage[1, half, pl.ds(x, 4, stride=N), :] = p_0[x + 4, half, 36:40, :]
    send_x(0)

    def forward(c):
        spread[c, 1, 0].wait_recv()
        cross(c, 1, gathered[c].at[mate, gx], gathered[c].at[mate, gx])
        for d, hop in enumerate(HOPS):
            spread[c, 0, hop].wait_recv()
            spread[c, 1, hop].wait_recv()
            z = lax.rem(gx + 4 - hop, 4)
            both = gathered[c].at[pl.ds(pair, 2), z]
            cross(c, d + 2, both, both)
        own[c].wait()

    def depth_term(t):
        values = jnp.concatenate([q[t][:, 0].reshape(N * N, 128), q[t][:, 1].reshape(N * N, 128)], axis=-1)
        hi = values.astype(jnp.bfloat16)
        lo = (values - hi.astype(jnp.float32)).astype(jnp.bfloat16)
        total = jnp.dot(hi, band_hi[...], preferred_element_type=jnp.float32)
        total = total + jnp.dot(lo, band_hi[...], preferred_element_type=jnp.float32)
        total = total + jnp.dot(hi, band_lo[...], preferred_element_type=jnp.float32)
        deep[:, 0] = total[:, :128].reshape(N, N, 128)
        deep[:, 1] = total[:, 128:].reshape(N, N, 128)

    def laplace(t, x, half):
        total = (2.0 * WEIGHTS[0]) * p[t][x + 4, half, 8:40, :]
        for k in range(1, 5):
            pair = p[t][x + 4 + k, half, 8:40, :] + p[t][x + 4 - k, half, 8:40, :]
            pair = pair + (p[t][x + 4, half, 8 + k:40 + k, :] + p[t][x + 4, half, 8 - k:40 - k, :])
            total = total + WEIGHTS[k] * pair
        return total

    bases = [lax.div(anchors[g], N) for g in shots]
    shifts = [lax.rem(anchors[g], N) for g in shots]
    shift = shifts[0]
    deal = {}

    def select(c):
        for piece in range(5):
            x_copy[c, piece].wait_recv()
        if c == CHUNKS - 1:
            send_y(0, 0)
            send_y(0, 1)
        for slot, (other, hop) in enumerate(PARTNERS + ((0, 0),)):
            z = lax.rem(gx + hop, 4)
            mine = (other, hop) == (0, 0)
            row = first_row[0] + PIECES[c][0]
            cells = pl.ds(PIECES[c][1], PIECES[c][2])
            at = jnp.minimum(bases[other] + z + (8 * gx + row < shifts[other]).astype(jnp.int32), 15)
            values = gathered[c][lax.div(at, 4), lax.rem(at, 4)]
            if mine:
                window[:, gx, row, cells] = values
            else:
                outgoing[slot, :, PIECES[c][0], cells] = values
                deal[c, slot] = pltpu.make_async_remote_copy(
                    src_ref=outgoing.at[slot, :, PIECES[c][0], cells],
                    dst_ref=window.at[:, gx, row, cells],
                    send_sem=deal_send.at[c, slot], recv_sem=deal_recv.at[c, slot],
                    device_id=to(shots[other], z, gy), device_id_type=MESH)
                deal[c, slot].start()

    def gains(c):
        for slot in range(7):
            deal[c, slot].wait_recv()

        @pl.loop(0, 8)
        def _(block):
            kk, y0, count = PIECES[c]
            cells = slice(y0, y0 + count)
            row = 4 * lax.rem(block, 2) + kk
            speed = window[0, lax.div(block, 2), row, cells].astype(jnp.float32)
            eps = window[1, lax.div(block, 2), row, cells].astype(jnp.float32)
            dlt = window[2, lax.div(block, 2), row, cells].astype(jnp.float32)
            square = speed * speed
            cross_term = square * jnp.sqrt(1.0 + 2.0 * dlt)
            horiz = square * (1.0 + 2.0 * eps)
            for half in range(2):
                z = slice(128 * half, 128 * half + 128)
                gain_a[4 * block + kk, half, cells] = horiz[:, z]
                gain_b[4 * block + kk, half, cells] = cross_term[:, z]
                gain_c[4 * block + kk, half, cells] = square[:, z]

    def first_depth():
        for i in range(5, len(loads)):
            loads[i].wait()
        depth_term(0)

    def first_lap():
        @pl.loop(0, N // 2)
        def _(pair):
            for u in range(2):
                for half in range(2):
                    lap[2 * pair + u, half] = laplace(0, 2 * pair + u, half)

        await_x(0)
        for side in range(2):
            for half in range(2):
                for i, value in enumerate(corrections(unpack_layers(x_in.at[0, side, half], side), side)):
                    lap[28 * side + i, half] = lap[28 * side + i, half] + value

    def first_y():
        await_y(0, 0)
        await_y(0, 1)

        @pl.loop(0, N)
        def _(x):
            for half in range(2):
                for side in range(2):
                    rows = slice(28 * side, 28 * side + 4)
                    lap[x, half, rows, :] = lap[x, half, rows, :] + corner[side, half, pl.ds(x, 4, stride=N), :]

    forward(0)
    forward(1)
    first_depth()
    forward(2)
    select(0)
    forward(3)
    forward(4)
    select(1)
    first_lap()
    gains(0)
    select(2)
    gains(1)
    select(3)
    select(4)
    gains(2)
    gains(3)
    gains(4)

    def step(t, do_p, do_q):
        before_p = p_m if t == 0 else p[t - 1]
        before_q = q_m if t == 0 else q[t - 1]
        off = 0 if t == 0 else 4
        y0 = 0 if t == 0 else 8
        last = t == STEPS - 1

        def plane(x):
            k = lax.rem(x + shift, N)
            amount = jnp.where(x + gx * N == sources[0, 0], wavelet[0, t], jnp.float32(0))
            for half in range(2):
                h = lap[x, half] if t == 0 else laplace(t, x, half)
                z = deep[x, half]
                b = gain_b[k, half]
                if do_p:
                    new_p = (2.0 * p[t][x + 4, half, 8:40, :] - before_p[x + off, half, y0:y0 + N, :]) + (
                        gain_a[k, half] * h + b * z)
                    new_p = new_p + amount * spot[half]
                    if last:
                        p_out[0, x, :, 128 * half:128 * half + 128] = new_p
                    else:
                        p[t + 1][x + 4, half, 8:40, :] = new_p
                    if t == 0:
                        stage[0, half, pl.ds(x, 4, stride=N), :] = new_p[0:4]
                        stage[1, half, pl.ds(x, 4, stride=N), :] = new_p[28:32]
                if do_q:
                    new_q = (2.0 * q[t][x, half] - before_q[x, half]) + (b * h + gain_c[k, half] * z)
                    if last:
                        q_out[0, x, :, 128 * half:128 * half + 128] = new_q
                    else:
                        q[t + 1][x, half] = new_q

        @pl.loop(0, N // 2)
        def _(pair):
            plane(2 * pair)
            plane(2 * pair + 1)

    def bump_p(t, x, k, half, first, count, value):
        rows = slice(first, first + count)
        add = gain_a[k, half, rows, :] * value
        if t == STEPS - 1:
            z = slice(128 * half, 128 * half + 128)
            p_out[0, x, rows, z] = p_out[0, x, rows, z] + add
        else:
            lower = slice(8 + first, 8 + first + count)
            new_p = p[t + 1][x + 4, half, lower, :] + add
            p[t + 1][x + 4, half, lower, :] = new_p

    def bump_q(t, x, k, half, first, count, value):
        rows = slice(first, first + count)
        add = gain_b[k, half, rows, :] * value
        if t == STEPS - 1:
            z = slice(128 * half, 128 * half + 128)
            q_out[0, x, rows, z] = q_out[0, x, rows, z] + add
        else:
            q[t + 1][x, half, rows, :] = q[t + 1][x, half, rows, :] + add

    def add_x(t, bumps):
        for side in range(2):
            for half in range(2):
                for i, value in enumerate(corrections(unpack_layers(x_in.at[t, side, half], side), side)):
                    x = 28 * side + i
                    for bump in bumps:
                        bump(t, x, lax.rem(x + shift, N), half, 0, N, value)

    def add_y(t, bumps, halves):
        @pl.loop(0, N // 2)
        def _(pair):
            for u in range(2):
                x = 2 * pair + u
                k = lax.rem(x + shift, N)
                for half in halves:
                    for side in range(2):
                        value = corner[side, half, pl.ds(x, 4, stride=N), :]
                        for bump in bumps:
                            bump(t, x, k, half, 28 * side, 4, value)

    def each_rim(move, first, last):
        @pl.loop(first, last)
        def _(x):
            for half in range(2):
                for side in range(2):
                    move(x, half, side)

    def keep_gain(x, half, side):
        face[side, half, pl.ds(x, 4, stride=N), :] = gain_a[lax.rem(x + shift, N), half, 28 * side:28 * side + 4, :]

    first_y()
    step(0, True, False)
    send_rims(1)
    each_rim(keep_gain, 0, N)
    step(0, False, True)
    for t in range(1, STEPS):
        depth_term(t)
        step(t, True, True)
        await_x(t)
        add_x(t, (bump_p, bump_q))
        if t == STEPS - 1:
            for half in range(2):
                await_y(t, half)
                add_y(t, (bump_p, bump_q), (half,))
            break

        def take(x, half, side):
            stage[side, half, pl.ds(x, 4, stride=N), :] = p[t + 1][x + 4, half, 8 + 28 * side:12 + 28 * side, :]

        def give(x, half, side):
            p[t + 1][x + 4, half, 8 + 28 * side:12 + 28 * side, :] = stage[side, half, pl.ds(x, 4, stride=N), :]

        each_rim(take, 0, N)
        for half in range(2):
            await_y(t, half)
            for side in range(2):
                stage[side, half] = stage[side, half] + face[side, half] * corner[side, half]
            send_y(t + 1, half)
        each_rim(give, 0, 4)
        each_rim(give, 28, 32)
        send_x(t + 1)
        each_rim(give, 4, 28)
        add_y(t, (bump_q,), (0, 1))

    for side in range(2):
        @pl.when(has_gx[side])
        def _():
            for t in range(STEPS):
                x_halo(t, side).wait_send()

        @pl.when(has_gy[side])
        def _():
            for t in range(STEPS):
                y_halo(t, side, 0).wait_send()
                y_halo(t, side, 1).wait_send()

    for c in range(CHUNKS):
        for slot, (other, hop) in enumerate(PARTNERS):
            spread[c, other, hop].wait_send()
            deal[c, slot].wait_send()
        for piece in range(5):
            x_copy[c, piece].wait_send()


def keep(p_in, q_in, p_out, q_out, sem):
    copies = [pltpu.make_async_copy(p_in, p_out, sem.at[0]), pltpu.make_async_copy(q_in, q_out, sem.at[1])]
    for copy in copies:
        copy.start()
    for copy in copies:
        copy.wait()


def on_device(velocity, epsilon, delta, anchors, sources, wavelet, p_now, p_prev, q_now, q_prev):
    out = pltpu.VMEM(p_now.shape, jnp.float32)
    vmem = pl.BlockSpec(memory_space=pltpu.VMEM)
    hbm = pl.BlockSpec(memory_space=pl.ANY)
    smem = pl.BlockSpec(memory_space=pltpu.SMEM)
    f32 = jnp.float32
    bf16 = jnp.bfloat16
    block = pltpu.VMEM((N, 2, N, 128), f32)
    padded = pltpu.VMEM((N + 8, 2, N + 16, 128), f32)
    rims = pltpu.VMEM((STEPS, 2, 2, 5, N, 128), bf16)
    dma = pltpu.SemaphoreType.DMA
    p_end, q_end = pl.pallas_call(
        kernel,
        out_shape=(out, out),
        in_specs=[hbm, hbm, hbm, smem, smem, smem, hbm, hbm, hbm, hbm],
        out_specs=(vmem, vmem),
        scratch_shapes=[
            pltpu.VMEM((3, N, N, 256), bf16),
            *[pltpu.VMEM((4, 4, 3, count, 256), bf16) for _, _, count in PIECES],
            pltpu.VMEM((7, 3, 4, N, 256), bf16),
            pltpu.VMEM((3, 4, 8, N, 256), bf16),
            block, block, block, block, block,
            pltpu.VMEM((256, 256), bf16), pltpu.VMEM((256, 256), bf16), pltpu.VMEM((2, N, 128), f32),
            block, padded, padded, padded, padded,
            block, block, block, block, block,
            pltpu.VMEM((2, 2, 4 * N, 128), f32), pltpu.VMEM((2, 2, 4 * N, 128), f32), pltpu.VMEM((2, 2, 4 * N, 128), f32),
            rims, rims, rims, rims,
            dma((11,)), dma((CHUNKS, 2, 4)), dma((CHUNKS, 2, 4)), dma((CHUNKS,)), dma((CHUNKS, 5)), dma((CHUNKS, 5)),
            dma((CHUNKS, 7)), dma((CHUNKS, 7)),
            dma((STEPS, 6)), dma((STEPS, 6)),
        ],
        compiler_params=pltpu.CompilerParams(
            collective_id=0, has_side_effects=True, vmem_limit_bytes=56 << 20),
        name="migrate",
    )(velocity, epsilon, delta, anchors, sources, wavelet, p_now, p_prev, q_now, q_prev)
    result = jax.ShapeDtypeStruct(p_now.shape, f32)
    return pl.pallas_call(
        keep,
        out_shape=(result, result),
        in_specs=[vmem, vmem],
        out_specs=(hbm, hbm),
        scratch_shapes=[dma((2,))],
        name="keep",
    )(pltpu.with_memory_space_constraint(p_end, pltpu.VMEM), pltpu.with_memory_space_constraint(q_end, pltpu.VMEM))


def solution(mesh):
    field = P("shot", "gx", "gy", None)
    model = P(("shot", "gx"), "gy", None)
    return jax.shard_map(
        on_device,
        mesh=mesh,
        in_specs=(model, model, model, P(), P("shot", None), P("shot", None), field, field, field, field),
        out_specs=(field, field),
        check_vma=False,
    )
```

```python
import jax
import jax.numpy as jnp
from jax import lax
from jax.experimental import pallas as pl
from jax.experimental.pallas import tpu as pltpu
from jax.sharding import PartitionSpec as P

STEPS = 4
WEIGHTS = (-205.0 / 72.0, 8.0 / 5.0, -1.0 / 5.0, 8.0 / 315.0, -1.0 / 560.0)
MESH = pl.DeviceIdType.MESH
N = 32
PIECES = ((0, 0, 32, 0, 3), (1, 0, 32, 0, 3), (2, 0, 32, 0, 3), (3, 0, 16, 0, 3), (3, 16, 16, 0, 2), (3, 16, 16, 2, 1))
CHUNKS = len(PIECES)
HOPS = (1, 3, 2)
PARTNERS = ((0, 1), (1, 1), (0, 3), (1, 3), (0, 2), (1, 2), (1, 0))


def kernel(
    velocity, epsilon, delta, anchors, sources, wavelet, p_now, p_prev, q_now, q_prev,
    p_out, q_out,
    slab, *scratch,
):
    gathered = scratch[:CHUNKS]
    (outgoing, window,
    gain_a, gain_b, gain_c, lap, deep, band_hi, band_lo, spot,
    p_m, p_0, p_1, p_2, p_3, q_m, q_0, q_1, q_2, q_3,
    stage, corner, face, x_out, x_in, y_out, y_in,
    load_sem, spread_send, spread_recv, own_sem, x_send, x_recv,
    deal_send, deal_recv, halo_send, halo_recv) = scratch[CHUNKS:]
    p = (p_0, p_1, p_2, p_3)
    q = (q_0, q_1, q_2, q_3)
    shot = lax.axis_index("shot")
    gx = lax.axis_index("gx")
    gy = lax.axis_index("gy")
    far = lax.rem(shot + 2, 4)
    mate = shot + 1 - 2 * lax.rem(shot, 2)
    core = lax.rem(shot, 2)
    pair = shot - core
    shots = (shot, mate)
    first_row = (4 * core, 4 - 4 * core)
    has_gx = (gx > 0, gx < 3)
    has_gy = (gy > 0, gy < 7)

    def to(s, z, y):
        return (s, z, y)

    barrier = pltpu.get_barrier_semaphore()
    for hop in HOPS:
        pl.semaphore_signal(barrier, inc=1, device_id=to(shot, lax.rem(gx + hop, 4), gy), device_id_type=MESH)
    pl.semaphore_signal(barrier, inc=1, device_id=to(far, gx, gy), device_id_type=MESH)
    for hop in range(4):
        pl.semaphore_signal(barrier, inc=1, device_id=to(mate, lax.rem(gx + hop, 4), gy), device_id_type=MESH)
    for side in range(2):
        @pl.when(has_gy[side])
        def _():
            pl.semaphore_signal(barrier, inc=1, device_id=to(shot, gx, gy + 2 * side - 1), device_id_type=MESH)

    loads = []
    def load(src, dst):
        copy = pltpu.make_async_copy(src, dst, load_sem.at[len(loads)])
        copy.start()
        loads.append(copy)
    for m, model in enumerate((velocity, epsilon, delta)):
        load(model, slab.at[m])
    for half in range(2):
        z = pl.ds(128 * half, 128)
        load(p_now.at[0, :, :, z], p_0.at[pl.ds(4, N), half, pl.ds(8, N), :])
    for src, dst in ((p_prev, p_m), (q_now, q_0), (q_prev, q_m)):
        for half in range(2):
            load(src.at[0, :, :, pl.ds(128 * half, 128)], dst.at[:, half])

    pl.semaphore_wait(barrier, 8 + has_gy[0].astype(jnp.int32) + has_gy[1].astype(jnp.int32))

    for m in range(3):
        loads[m].wait()
    spread = {}
    x_copy = {}
    def scatter(c):
        for other, hop in PARTNERS:
            z = lax.rem(gx + hop, 4)
            spread[c, other, hop] = pltpu.make_async_remote_copy(
                src_ref=slab.at[pl.ds(PIECES[c][3], PIECES[c][4]), 8 * z + first_row[other] + PIECES[c][0], pl.ds(PIECES[c][1], PIECES[c][2])],
                dst_ref=gathered[c].at[shot, gx],
                send_sem=spread_send.at[c, other, hop], recv_sem=spread_recv.at[c, other, hop],
                device_id=to(shots[other], z, gy), device_id_type=MESH)
            spread[c, other, hop].start()

    def cross(c, piece, src, dst):
        x_copy[c, piece] = pltpu.make_async_remote_copy(
            src_ref=src, dst_ref=dst, send_sem=x_send.at[c, piece], recv_sem=x_recv.at[c, piece],
            device_id=to(far, gx, gy), device_id_type=MESH)
        x_copy[c, piece].start()

    def own_rows(c):
        return slab.at[pl.ds(PIECES[c][3], PIECES[c][4]), 8 * gx + first_row[0] + PIECES[c][0], pl.ds(PIECES[c][1], PIECES[c][2])]

    for c in range(CHUNKS):
        cross(c, 0, own_rows(c), gathered[c].at[shot, gx])
    for c in range(CHUNKS):
        scatter(c)
    own = []
    for c in range(CHUNKS):
        own.append(pltpu.make_async_copy(own_rows(c), gathered[c].at[shot, gx], own_sem.at[c]))
        own[c].start()

    def x_halo(t, side):
        return pltpu.make_async_remote_copy(
            src_ref=x_out.at[t, side], dst_ref=x_in.at[t, 1 - side],
            send_sem=halo_send.at[t, side], recv_sem=halo_recv.at[t, side],
            device_id=to(shot, gx + 2 * side - 1, gy), device_id_type=MESH)

    def y_halo(t, side, half):
        return pltpu.make_async_remote_copy(
            src_ref=y_out.at[t, side, half], dst_ref=y_in.at[t, 1 - side, half],
            send_sem=halo_send.at[t, 2 + 2 * side + half], recv_sem=halo_recv.at[t, 2 + 2 * side + half],
            device_id=to(shot, gx, gy + 2 * side - 1), device_id_type=MESH)

    def pack_layers(out, side, layer, values):
        near = 3 if side else 0
        hi = values.astype(jnp.bfloat16)
        out[layer] = hi
        if layer == near:
            out[4] = (values - hi.astype(jnp.float32)).astype(jnp.bfloat16)

    def unpack_layers(source, side):
        near = 0 if side else 3
        layers = [source[layer].astype(jnp.float32) for layer in range(4)]
        layers[near] = layers[near] + source[4].astype(jnp.float32)
        return layers

    def corrections(layers, side):
        result = []
        for i in range(4):
            reach = range(i + 1) if side else range(i, 4)
            terms = [WEIGHTS[4 + j - i if side else i + 4 - j] * layers[j] for j in reach]
            total = terms[0]
            for term in terms[1:]:
                total = total + term
            result.append(total)
        return result

    def send_y(t, half):
        for side in range(2):
            for layer in range(4):
                pack_layers(y_out.at[t, side, half], side, layer, stage[side, half, N * layer:N * layer + N, :])

            @pl.when(has_gy[side])
            def _():
                y_halo(t, side, half).start()

    def send_x(t):
        for side in range(2):
            for half in range(2):
                for layer in range(4):
                    pack_layers(x_out.at[t, side, half], side, layer, p[t][4 + 28 * side + layer, half, 8:40, :])
            @pl.when(has_gx[side])
            def _():
                x_halo(t, side).start()

    def await_x(t):
        for side in range(2):
            @pl.when(has_gx[side])
            def _():
                x_halo(t, 1 - side).wait_recv()

    def await_y(t, half):
        for side in range(2):
            @pl.when(has_gy[side])
            def _():
                y_halo(t, 1 - side, half).wait_recv()
        for side in range(2):
            for i, value in enumerate(corrections(unpack_layers(y_in.at[t, side, half], side), side)):
                corner[side, half, N * i:N * i + N, :] = value

    for side in range(2):
        @pl.when(jnp.logical_not(has_gx[side]))
        def _():
            for t in range(STEPS):
                x_in[t, side] = jnp.zeros((2, 5, N, 128), jnp.bfloat16)

        @pl.when(jnp.logical_not(has_gy[side]))
        def _():
            for t in range(STEPS):
                y_in[t, side] = jnp.zeros((2, 5, N, 128), jnp.bfloat16)

    for t in range(STEPS):
        @pl.loop(0, 4)
        def _(x):
            for half in range(2):
                p[t][x, half, 8:40, :] = jnp.zeros((N, 128), jnp.float32)
                p[t][x + 36, half, 8:40, :] = jnp.zeros((N, 128), jnp.float32)

        @pl.loop(0, N)
        def _(x):
            for half in range(2):
                p[t][x + 4, half, 0:8, :] = jnp.zeros((8, 128), jnp.float32)
                p[t][x + 4, half, 40:48, :] = jnp.zeros((8, 128), jnp.float32)

    row = lax.broadcasted_iota(jnp.int32, (256, 256), 0)
    col = lax.broadcasted_iota(jnp.int32, (256, 256), 1)
    apart = jnp.abs(row - col)
    band = jnp.zeros((256, 256), jnp.float32)
    for k in range(5):
        band = jnp.where(apart == k, jnp.float32(WEIGHTS[k]), band)
    hi = band.astype(jnp.bfloat16)
    band_hi[...] = hi
    band_lo[...] = (band - hi.astype(jnp.float32)).astype(jnp.bfloat16)
    y_at = lax.broadcasted_iota(jnp.int32, (N, 128), 0) + gy * N
    z_at = lax.broadcasted_iota(jnp.int32, (N, 128), 1)
    for half in range(2):
        here = jnp.logical_and(y_at == sources[0, 1], z_at + 128 * half == sources[0, 2])
        spot[half] = jnp.where(here, jnp.float32(1), jnp.float32(0))

    for i in range(3, 5):
        loads[i].wait()

    @pl.loop(0, N)
    def _(x):
        for half in range(2):
            stage[0, half, pl.ds(x, 4, stride=N), :] = p_0[x + 4, half, 8:12, :]
            stage[1, half, pl.ds(x, 4, stride=N), :] = p_0[x + 4, half, 36:40, :]
    send_x(0)

    def forward(c):
        spread[c, 1, 0].wait_recv()
        cross(c, 1, gathered[c].at[mate, gx], gathered[c].at[mate, gx])
        for d, hop in enumerate(HOPS):
            spread[c, 0, hop].wait_recv()
            spread[c, 1, hop].wait_recv()
            z = lax.rem(gx + 4 - hop, 4)
            both = gathered[c].at[pl.ds(pair, 2), z]
            cross(c, d + 2, both, both)
        own[c].wait()

    def depth_term(t):
        values = jnp.concatenate([q[t][:, 0].reshape(N * N, 128), q[t][:, 1].reshape(N * N, 128)], axis=-1)
        hi = values.astype(jnp.bfloat16)
        lo = (values - hi.astype(jnp.float32)).astype(jnp.bfloat16)
        total = jnp.dot(hi, band_hi[...], preferred_element_type=jnp.float32)
        total = total + jnp.dot(lo, band_hi[...], preferred_element_type=jnp.float32)
        total = total + jnp.dot(hi, band_lo[...], preferred_element_type=jnp.float32)
        deep[:, 0] = total[:, :128].reshape(N, N, 128)
        deep[:, 1] = total[:, 128:].reshape(N, N, 128)

    def laplace(t, x, half):
        total = (2.0 * WEIGHTS[0]) * p[t][x + 4, half, 8:40, :]
        for k in range(1, 5):
            pair = p[t][x + 4 + k, half, 8:40, :] + p[t][x + 4 - k, half, 8:40, :]
            pair = pair + (p[t][x + 4, half, 8 + k:40 + k, :] + p[t][x + 4, half, 8 - k:40 - k, :])
            total = total + WEIGHTS[k] * pair
        return total

    bases = [lax.div(anchors[g], N) for g in shots]
    shifts = [lax.rem(anchors[g], N) for g in shots]
    shift = shifts[0]
    deal = {}

    def select(c):
        for piece in range(5):
            x_copy[c, piece].wait_recv()
        if c == CHUNKS - 2:
            send_y(0, 0)
            send_y(0, 1)
        for slot, (other, hop) in enumerate(PARTNERS + ((0, 0),)):
            z = lax.rem(gx + hop, 4)
            mine = (other, hop) == (0, 0)
            row = first_row[0] + PIECES[c][0]
            cells = pl.ds(PIECES[c][1], PIECES[c][2])
            models = pl.ds(PIECES[c][3], PIECES[c][4])
            at = jnp.minimum(bases[other] + z + (8 * gx + row < shifts[other]).astype(jnp.int32), 15)
            values = gathered[c][lax.div(at, 4), lax.rem(at, 4)]
            if mine:
                window[models, gx, row, cells] = values
            else:
                outgoing[slot, models, PIECES[c][0], cells] = values
                deal[c, slot] = pltpu.make_async_remote_copy(
                    src_ref=outgoing.at[slot, models, PIECES[c][0], cells],
                    dst_ref=window.at[models, gx, row, cells],
                    send_sem=deal_send.at[c, slot], recv_sem=deal_recv.at[c, slot],
                    device_id=to(shots[other], z, gy), device_id_type=MESH)
                deal[c, slot].start()

    def gains(c):
        for slot in range(7):
            deal[c, slot].wait_recv()
        if PIECES[c][3] + PIECES[c][4] < 3:
            return

        @pl.loop(0, 8)
        def _(block):
            kk, y0, count = PIECES[c][:3]
            cells = slice(y0, y0 + count)
            row = 4 * lax.rem(block, 2) + kk
            speed = window[0, lax.div(block, 2), row, cells].astype(jnp.float32)
            eps = window[1, lax.div(block, 2), row, cells].astype(jnp.float32)
            dlt = window[2, lax.div(block, 2), row, cells].astype(jnp.float32)
            square = speed * speed
            cross_term = square * jnp.sqrt(1.0 + 2.0 * dlt)
            horiz = square * (1.0 + 2.0 * eps)
            for half in range(2):
                z = slice(128 * half, 128 * half + 128)
                gain_a[4 * block + kk, half, cells] = horiz[:, z]
                gain_b[4 * block + kk, half, cells] = cross_term[:, z]
                gain_c[4 * block + kk, half, cells] = square[:, z]

    def first_depth():
        for i in range(5, len(loads)):
            loads[i].wait()
        depth_term(0)

    def first_lap():
        @pl.loop(0, N // 2)
        def _(pair):
            for u in range(2):
                for half in range(2):
                    lap[2 * pair + u, half] = laplace(0, 2 * pair + u, half)

        await_x(0)
        for side in range(2):
            for half in range(2):
                for i, value in enumerate(corrections(unpack_layers(x_in.at[0, side, half], side), side)):
                    lap[28 * side + i, half] = lap[28 * side + i, half] + value

    forward(0)
    forward(1)
    first_depth()
    forward(2)
    select(0)
    forward(3)
    forward(4)
    forward(5)
    select(1)
    first_lap()
    gains(0)
    select(2)
    gains(1)
    select(3)
    select(4)
    select(5)
    gains(2)
    gains(3)
    gains(4)
    gains(5)

    def step(t, do_p, do_q):
        before_p = p_m if t == 0 else p[t - 1]
        before_q = q_m if t == 0 else q[t - 1]
        off = 0 if t == 0 else 4
        y0 = 0 if t == 0 else 8
        last = t == STEPS - 1

        def plane(x):
            k = lax.rem(x + shift, N)
            amount = jnp.where(x + gx * N == sources[0, 0], wavelet[0, t], jnp.float32(0))
            for half in range(2):
                h = lap[x, half] if t == 0 else laplace(t, x, half)
                z = deep[x, half]
                b = gain_b[k, half]
                if do_p:
                    new_p = (2.0 * p[t][x + 4, half, 8:40, :] - before_p[x + off, half, y0:y0 + N, :]) + (
                        gain_a[k, half] * h + b * z)
                    new_p = new_p + amount * spot[half]
                    if last:
                        p_out[0, x, :, 128 * half:128 * half + 128] = new_p
                    else:
                        p[t + 1][x + 4, half, 8:40, :] = new_p
                    if t == 0:
                        stage[0, half, pl.ds(x, 4, stride=N), :] = new_p[0:4]
                        stage[1, half, pl.ds(x, 4, stride=N), :] = new_p[28:32]
                if do_q:
                    new_q = (2.0 * q[t][x, half] - before_q[x, half]) + (b * h + gain_c[k, half] * z)
                    if last:
                        q_out[0, x, :, 128 * half:128 * half + 128] = new_q
                    else:
                        q[t + 1][x, half] = new_q

        @pl.loop(0, N // 2)
        def _(pair):
            plane(2 * pair)
            plane(2 * pair + 1)

    def bump_p(t, x, k, half, first, count, value):
        rows = slice(first, first + count)
        add = gain_a[k, half, rows, :] * value
        if t == STEPS - 1:
            z = slice(128 * half, 128 * half + 128)
            p_out[0, x, rows, z] = p_out[0, x, rows, z] + add
        else:
            lower = slice(8 + first, 8 + first + count)
            new_p = p[t + 1][x + 4, half, lower, :] + add
            p[t + 1][x + 4, half, lower, :] = new_p

    def bump_q(t, x, k, half, first, count, value):
        rows = slice(first, first + count)
        add = gain_b[k, half, rows, :] * value
        if t == STEPS - 1:
            z = slice(128 * half, 128 * half + 128)
            q_out[0, x, rows, z] = q_out[0, x, rows, z] + add
        else:
            q[t + 1][x, half, rows, :] = q[t + 1][x, half, rows, :] + add

    def add_x(t, bumps):
        for side in range(2):
            for half in range(2):
                for i, value in enumerate(corrections(unpack_layers(x_in.at[t, side, half], side), side)):
                    x = 28 * side + i
                    for bump in bumps:
                        bump(t, x, lax.rem(x + shift, N), half, 0, N, value)

    def add_y(t, bumps, halves):
        @pl.loop(0, N // 2)
        def _(pair):
            for u in range(2):
                x = 2 * pair + u
                k = lax.rem(x + shift, N)
                for half in halves:
                    for side in range(2):
                        value = corner[side, half, pl.ds(x, 4, stride=N), :]
                        for bump in bumps:
                            bump(t, x, k, half, 28 * side, 4, value)

    def each_rim(move, first, last):
        @pl.loop(first, last)
        def _(x):
            for half in range(2):
                for side in range(2):
                    move(x, half, side)

    def keep_gain(x, half, side):
        face[side, half, pl.ds(x, 4, stride=N), :] = gain_a[lax.rem(x + shift, N), half, 28 * side:28 * side + 4, :]

    def pass_on(t):
        def give(x, half, side):
            p[t + 1][x + 4, half, 8 + 28 * side:12 + 28 * side, :] = stage[side, half, pl.ds(x, 4, stride=N), :]

        for half in range(2):
            await_y(t, half)
            for side in range(2):
                stage[side, half] = stage[side, half] + face[side, half] * corner[side, half]
            send_y(t + 1, half)
        each_rim(give, 0, 4)
        each_rim(give, 28, 32)
        send_x(t + 1)
        each_rim(give, 4, 28)

    step(0, True, False)
    each_rim(keep_gain, 0, N)
    pass_on(0)
    step(0, False, True)
    add_y(0, (bump_q,), (0, 1))
    for t in range(1, STEPS):
        depth_term(t)
        step(t, True, True)
        await_x(t)
        add_x(t, (bump_p, bump_q))
        if t == STEPS - 1:
            for half in range(2):
                await_y(t, half)
                add_y(t, (bump_p, bump_q), (half,))
            break

        def take(x, half, side):
            stage[side, half, pl.ds(x, 4, stride=N), :] = p[t + 1][x + 4, half, 8 + 28 * side:12 + 28 * side, :]

        each_rim(take, 0, N)
        pass_on(t)
        add_y(t, (bump_q,), (0, 1))

    for side in range(2):
        @pl.when(has_gx[side])
        def _():
            for t in range(STEPS):
                x_halo(t, side).wait_send()

        @pl.when(has_gy[side])
        def _():
            for t in range(STEPS):
                y_halo(t, side, 0).wait_send()
                y_halo(t, side, 1).wait_send()

    for c in range(CHUNKS):
        for slot, (other, hop) in enumerate(PARTNERS):
            spread[c, other, hop].wait_send()
            deal[c, slot].wait_send()
        for piece in range(5):
            x_copy[c, piece].wait_send()


def keep(p_in, q_in, p_out, q_out, sem):
    copies = [pltpu.make_async_copy(p_in, p_out, sem.at[0]), pltpu.make_async_copy(q_in, q_out, sem.at[1])]
    for copy in copies:
        copy.start()
    for copy in copies:
        copy.wait()


def on_device(velocity, epsilon, delta, anchors, sources, wavelet, p_now, p_prev, q_now, q_prev):
    out = pltpu.VMEM(p_now.shape, jnp.float32)
    vmem = pl.BlockSpec(memory_space=pltpu.VMEM)
    hbm = pl.BlockSpec(memory_space=pl.ANY)
    smem = pl.BlockSpec(memory_space=pltpu.SMEM)
    f32 = jnp.float32
    bf16 = jnp.bfloat16
    block = pltpu.VMEM((N, 2, N, 128), f32)
    padded = pltpu.VMEM((N + 8, 2, N + 16, 128), f32)
    rims = pltpu.VMEM((STEPS, 2, 2, 5, N, 128), bf16)
    dma = pltpu.SemaphoreType.DMA
    p_end, q_end = pl.pallas_call(
        kernel,
        out_shape=(out, out),
        in_specs=[hbm, hbm, hbm, smem, smem, smem, hbm, hbm, hbm, hbm],
        out_specs=(vmem, vmem),
        scratch_shapes=[
            pltpu.VMEM((3, N, N, 256), bf16),
            *[pltpu.VMEM((4, 4, models, count, 256), bf16) for _, _, count, _, models in PIECES],
            pltpu.VMEM((7, 3, 4, N, 256), bf16),
            pltpu.VMEM((3, 4, 8, N, 256), bf16),
            block, block, block, block, block,
            pltpu.VMEM((256, 256), bf16), pltpu.VMEM((256, 256), bf16), pltpu.VMEM((2, N, 128), f32),
            block, padded, padded, padded, padded,
            block, block, block, block, block,
            pltpu.VMEM((2, 2, 4 * N, 128), f32), pltpu.VMEM((2, 2, 4 * N, 128), f32), pltpu.VMEM((2, 2, 4 * N, 128), f32),
            rims, rims, rims, rims,
            dma((11,)), dma((CHUNKS, 2, 4)), dma((CHUNKS, 2, 4)), dma((CHUNKS,)), dma((CHUNKS, 5)), dma((CHUNKS, 5)),
            dma((CHUNKS, 7)), dma((CHUNKS, 7)),
            dma((STEPS, 6)), dma((STEPS, 6)),
        ],
        compiler_params=pltpu.CompilerParams(
            collective_id=0, has_side_effects=True, vmem_limit_bytes=56 << 20),
        name="migrate",
    )(velocity, epsilon, delta, anchors, sources, wavelet, p_now, p_prev, q_now, q_prev)
    result = jax.ShapeDtypeStruct(p_now.shape, f32)
    return pl.pallas_call(
        keep,
        out_shape=(result, result),
        in_specs=[vmem, vmem],
        out_specs=(hbm, hbm),
        scratch_shapes=[dma((2,))],
        name="keep",
    )(pltpu.with_memory_space_constraint(p_end, pltpu.VMEM), pltpu.with_memory_space_constraint(q_end, pltpu.VMEM))


def solution(mesh):
    field = P("shot", "gx", "gy", None)
    model = P(("shot", "gx"), "gy", None)
    return jax.shard_map(
        on_device,
        mesh=mesh,
        in_specs=(model, model, model, P(), P("shot", None), P("shot", None), field, field, field, field),
        out_specs=(field, field),
        check_vma=False,
    )
```

```python
import jax
import jax.numpy as jnp
from jax import lax
from jax.experimental import pallas as pl
from jax.experimental.pallas import tpu as pltpu
from jax.sharding import PartitionSpec as P

STEPS = 4
WEIGHTS = (-205.0 / 72.0, 8.0 / 5.0, -1.0 / 5.0, 8.0 / 315.0, -1.0 / 560.0)
MESH = pl.DeviceIdType.MESH
N = 32
PIECES = ((0, 0, 32, 0, 3), (1, 0, 32, 0, 3), (2, 0, 32, 0, 3), (3, 0, 16, 0, 3), (3, 16, 16, 0, 2), (3, 16, 16, 2, 1))
CHUNKS = len(PIECES)
HOPS = (1, 3, 2)
PARTNERS = ((0, 1), (1, 1), (0, 3), (1, 3), (0, 2), (1, 2), (1, 0))


def kernel(
    velocity, epsilon, delta, anchors, sources, wavelet, p_now, p_prev, q_now, q_prev,
    p_out, q_out,
    slab, *scratch,
):
    gathered = scratch[:CHUNKS]
    (outgoing, window,
    gain_a, gain_b, gain_c, lap, deep, band_hi, band_lo, spot,
    p_m, p_0, p_1, p_2, p_3, q_m, q_0, q_1, q_2, q_3,
    stage, corner, face, x_out, x_in, y_out, y_in,
    load_sem, spread_send, spread_recv, own_sem, x_send, x_recv,
    deal_send, deal_recv, halo_send, halo_recv) = scratch[CHUNKS:]
    p = (p_0, p_1, p_2, p_3)
    q = (q_0, q_1, q_2, q_3)
    shot = lax.axis_index("shot")
    gx = lax.axis_index("gx")
    gy = lax.axis_index("gy")
    far = lax.rem(shot + 2, 4)
    mate = shot + 1 - 2 * lax.rem(shot, 2)
    core = lax.rem(shot, 2)
    pair = shot - core
    shots = (shot, mate)
    first_row = (4 * core, 4 - 4 * core)
    has_gx = (gx > 0, gx < 3)
    has_gy = (gy > 0, gy < 7)

    def to(s, z, y):
        return (s, z, y)

    barrier = pltpu.get_barrier_semaphore()
    for hop in HOPS:
        pl.semaphore_signal(barrier, inc=1, device_id=to(shot, lax.rem(gx + hop, 4), gy), device_id_type=MESH)
    pl.semaphore_signal(barrier, inc=1, device_id=to(far, gx, gy), device_id_type=MESH)
    for hop in range(4):
        pl.semaphore_signal(barrier, inc=1, device_id=to(mate, lax.rem(gx + hop, 4), gy), device_id_type=MESH)
    for side in range(2):
        @pl.when(has_gy[side])
        def _():
            pl.semaphore_signal(barrier, inc=1, device_id=to(shot, gx, gy + 2 * side - 1), device_id_type=MESH)

    loads = []
    def load(src, dst):
        copy = pltpu.make_async_copy(src, dst, load_sem.at[len(loads)])
        copy.start()
        loads.append(copy)
    for m, model in enumerate((velocity, epsilon, delta)):
        load(model, slab.at[m])
    for half in range(2):
        z = pl.ds(128 * half, 128)
        load(p_now.at[0, :, :, z], p_0.at[pl.ds(4, N), half, pl.ds(8, N), :])
    for src, dst in ((p_prev, p_m), (q_now, q_0), (q_prev, q_m)):
        for half in range(2):
            load(src.at[0, :, :, pl.ds(128 * half, 128)], dst.at[:, half])

    pl.semaphore_wait(barrier, 8 + has_gy[0].astype(jnp.int32) + has_gy[1].astype(jnp.int32))

    for m in range(3):
        loads[m].wait()
    spread = {}
    x_copy = {}
    def scatter(c):
        for other, hop in PARTNERS:
            z = lax.rem(gx + hop, 4)
            spread[c, other, hop] = pltpu.make_async_remote_copy(
                src_ref=slab.at[pl.ds(PIECES[c][3], PIECES[c][4]), 8 * z + first_row[other] + PIECES[c][0], pl.ds(PIECES[c][1], PIECES[c][2])],
                dst_ref=gathered[c].at[shot, gx],
                send_sem=spread_send.at[c, other, hop], recv_sem=spread_recv.at[c, other, hop],
                device_id=to(shots[other], z, gy), device_id_type=MESH)
            spread[c, other, hop].start()

    def cross(c, piece, src, dst):
        x_copy[c, piece] = pltpu.make_async_remote_copy(
            src_ref=src, dst_ref=dst, send_sem=x_send.at[c, piece], recv_sem=x_recv.at[c, piece],
            device_id=to(far, gx, gy), device_id_type=MESH)
        x_copy[c, piece].start()

    def own_rows(c):
        return slab.at[pl.ds(PIECES[c][3], PIECES[c][4]), 8 * gx + first_row[0] + PIECES[c][0], pl.ds(PIECES[c][1], PIECES[c][2])]

    for c in range(CHUNKS):
        cross(c, 0, own_rows(c), gathered[c].at[shot, gx])
    for c in range(CHUNKS):
        scatter(c)
    own = []
    for c in range(CHUNKS):
        own.append(pltpu.make_async_copy(own_rows(c), gathered[c].at[shot, gx], own_sem.at[c]))
        own[c].start()

    def x_halo(t, side):
        return pltpu.make_async_remote_copy(
            src_ref=x_out.at[t, side], dst_ref=x_in.at[t, 1 - side],
            send_sem=halo_send.at[t, side], recv_sem=halo_recv.at[t, side],
            device_id=to(shot, gx + 2 * side - 1, gy), device_id_type=MESH)

    def y_halo(t, side, half):
        return pltpu.make_async_remote_copy(
            src_ref=y_out.at[t, side, half], dst_ref=y_in.at[t, 1 - side, half],
            send_sem=halo_send.at[t, 2 + 2 * side + half], recv_sem=halo_recv.at[t, 2 + 2 * side + half],
            device_id=to(shot, gx, gy + 2 * side - 1), device_id_type=MESH)

    def pack_layers(out, side, layer, values):
        near = 3 if side else 0
        hi = values.astype(jnp.bfloat16)
        out[layer] = hi
        if layer == near:
            out[4] = (values - hi.astype(jnp.float32)).astype(jnp.bfloat16)

    def unpack_layers(source, side):
        near = 0 if side else 3
        layers = [source[layer].astype(jnp.float32) for layer in range(4)]
        layers[near] = layers[near] + source[4].astype(jnp.float32)
        return layers

    def corrections(layers, side):
        result = []
        for i in range(4):
            reach = range(i + 1) if side else range(i, 4)
            terms = [WEIGHTS[4 + j - i if side else i + 4 - j] * layers[j] for j in reach]
            total = terms[0]
            for term in terms[1:]:
                total = total + term
            result.append(total)
        return result

    def send_y(t, half):
        for side in range(2):
            for layer in range(4):
                pack_layers(y_out.at[t, side, half], side, layer, stage[side, half, N * layer:N * layer + N, :])

            @pl.when(has_gy[side])
            def _():
                y_halo(t, side, half).start()

    def send_x(t):
        for side in range(2):
            for half in range(2):
                for layer in range(4):
                    pack_layers(x_out.at[t, side, half], side, layer, p[t][4 + 28 * side + layer, half, 8:40, :])
            @pl.when(has_gx[side])
            def _():
                x_halo(t, side).start()

    def await_x(t):
        for side in range(2):
            @pl.when(has_gx[side])
            def _():
                x_halo(t, 1 - side).wait_recv()

    def await_y(t, half):
        for side in range(2):
            @pl.when(has_gy[side])
            def _():
                y_halo(t, 1 - side, half).wait_recv()
        for side in range(2):
            for i, value in enumerate(corrections(unpack_layers(y_in.at[t, side, half], side), side)):
                corner[side, half, N * i:N * i + N, :] = value

    for side in range(2):
        @pl.when(jnp.logical_not(has_gx[side]))
        def _():
            for t in range(STEPS):
                x_in[t, side] = jnp.zeros((2, 5, N, 128), jnp.bfloat16)

        @pl.when(jnp.logical_not(has_gy[side]))
        def _():
            for t in range(STEPS):
                y_in[t, side] = jnp.zeros((2, 5, N, 128), jnp.bfloat16)

    for t in range(STEPS):
        @pl.loop(0, 4)
        def _(x):
            for half in range(2):
                p[t][x, half, 8:40, :] = jnp.zeros((N, 128), jnp.float32)
                p[t][x + 36, half, 8:40, :] = jnp.zeros((N, 128), jnp.float32)

        @pl.loop(0, N)
        def _(x):
            for half in range(2):
                p[t][x + 4, half, 0:8, :] = jnp.zeros((8, 128), jnp.float32)
                p[t][x + 4, half, 40:48, :] = jnp.zeros((8, 128), jnp.float32)

    row = lax.broadcasted_iota(jnp.int32, (256, 256), 0)
    col = lax.broadcasted_iota(jnp.int32, (256, 256), 1)
    apart = jnp.abs(row - col)
    band = jnp.zeros((256, 256), jnp.float32)
    for k in range(5):
        band = jnp.where(apart == k, jnp.float32(WEIGHTS[k]), band)
    hi = band.astype(jnp.bfloat16)
    band_hi[...] = hi
    band_lo[...] = (band - hi.astype(jnp.float32)).astype(jnp.bfloat16)
    y_at = lax.broadcasted_iota(jnp.int32, (N, 128), 0) + gy * N
    z_at = lax.broadcasted_iota(jnp.int32, (N, 128), 1)
    for half in range(2):
        here = jnp.logical_and(y_at == sources[0, 1], z_at + 128 * half == sources[0, 2])
        spot[half] = jnp.where(here, jnp.float32(1), jnp.float32(0))

    for i in range(3, 5):
        loads[i].wait()

    @pl.loop(0, N)
    def _(x):
        for half in range(2):
            stage[0, half, pl.ds(x, 4, stride=N), :] = p_0[x + 4, half, 8:12, :]
            stage[1, half, pl.ds(x, 4, stride=N), :] = p_0[x + 4, half, 36:40, :]
    send_x(0)

    def forward(c):
        spread[c, 1, 0].wait_recv()
        cross(c, 1, gathered[c].at[mate, gx], gathered[c].at[mate, gx])
        for d, hop in enumerate(HOPS):
            spread[c, 0, hop].wait_recv()
            spread[c, 1, hop].wait_recv()
            z = lax.rem(gx + 4 - hop, 4)
            both = gathered[c].at[pl.ds(pair, 2), z]
            cross(c, d + 2, both, both)
        own[c].wait()

    def depth_term(t):
        values = jnp.concatenate([q[t][:, 0].reshape(N * N, 128), q[t][:, 1].reshape(N * N, 128)], axis=-1)
        hi = values.astype(jnp.bfloat16)
        lo = (values - hi.astype(jnp.float32)).astype(jnp.bfloat16)
        total = jnp.dot(hi, band_hi[...], preferred_element_type=jnp.float32)
        total = total + jnp.dot(lo, band_hi[...], preferred_element_type=jnp.float32)
        total = total + jnp.dot(hi, band_lo[...], preferred_element_type=jnp.float32)
        deep[:, 0] = total[:, :128].reshape(N, N, 128)
        deep[:, 1] = total[:, 128:].reshape(N, N, 128)

    def laplace(t, x, half):
        total = (2.0 * WEIGHTS[0]) * p[t][x + 4, half, 8:40, :]
        for k in range(1, 5):
            pair = p[t][x + 4 + k, half, 8:40, :] + p[t][x + 4 - k, half, 8:40, :]
            pair = pair + (p[t][x + 4, half, 8 + k:40 + k, :] + p[t][x + 4, half, 8 - k:40 - k, :])
            total = total + WEIGHTS[k] * pair
        return total

    bases = [lax.div(anchors[g], N) for g in shots]
    shifts = [lax.rem(anchors[g], N) for g in shots]
    shift = shifts[0]
    deal = {}

    def select(c):
        for piece in range(5):
            x_copy[c, piece].wait_recv()
        if c == CHUNKS - 2:
            send_y(0, 0)
            send_y(0, 1)
        for slot, (other, hop) in enumerate(PARTNERS + ((0, 0),)):
            z = lax.rem(gx + hop, 4)
            mine = (other, hop) == (0, 0)
            row = first_row[0] + PIECES[c][0]
            cells = pl.ds(PIECES[c][1], PIECES[c][2])
            models = pl.ds(PIECES[c][3], PIECES[c][4])
            at = jnp.minimum(bases[other] + z + (8 * gx + row < shifts[other]).astype(jnp.int32), 15)
            values = gathered[c][lax.div(at, 4), lax.rem(at, 4)]
            if mine:
                window[models, gx, row, cells] = values
            else:
                outgoing[slot, models, PIECES[c][0], cells] = values
                deal[c, slot] = pltpu.make_async_remote_copy(
                    src_ref=outgoing.at[slot, models, PIECES[c][0], cells],
                    dst_ref=window.at[models, gx, row, cells],
                    send_sem=deal_send.at[c, slot], recv_sem=deal_recv.at[c, slot],
                    device_id=to(shots[other], z, gy), device_id_type=MESH)
                deal[c, slot].start()

    def gains(c):
        for slot in range(7):
            deal[c, slot].wait_recv()
        if PIECES[c][3] + PIECES[c][4] < 3:
            return

        def gain_rows(block):
            kk, y0, count = PIECES[c][:3]
            cells = slice(y0, y0 + count)
            row = 4 * lax.rem(block, 2) + kk
            speed = window[0, lax.div(block, 2), row, cells].astype(jnp.float32)
            eps = window[1, lax.div(block, 2), row, cells].astype(jnp.float32)
            dlt = window[2, lax.div(block, 2), row, cells].astype(jnp.float32)
            square = speed * speed
            cross_term = square * jnp.sqrt(1.0 + 2.0 * dlt)
            horiz = square * (1.0 + 2.0 * eps)
            for half in range(2):
                z = slice(128 * half, 128 * half + 128)
                gain_a[4 * block + kk, half, cells] = horiz[:, z]
                gain_b[4 * block + kk, half, cells] = cross_term[:, z]
                gain_c[4 * block + kk, half, cells] = square[:, z]

        @pl.loop(0, 2)
        def _(group):
            for u in range(4):
                gain_rows(4 * group + u)

    def first_depth():
        for i in range(5, len(loads)):
            loads[i].wait()
        depth_term(0)

    def first_lap():
        @pl.loop(0, N // 2)
        def _(pair):
            for u in range(2):
                for half in range(2):
                    lap[2 * pair + u, half] = laplace(0, 2 * pair + u, half)

        await_x(0)
        for side in range(2):
            for half in range(2):
                for i, value in enumerate(corrections(unpack_layers(x_in.at[0, side, half], side), side)):
                    lap[28 * side + i, half] = lap[28 * side + i, half] + value

    forward(0)
    forward(1)
    first_depth()
    forward(2)
    select(0)
    forward(3)
    forward(4)
    forward(5)
    select(1)
    first_lap()
    gains(0)
    select(2)
    gains(1)
    select(3)
    select(4)
    select(5)
    gains(2)
    gains(3)
    gains(4)
    gains(5)

    def step(t, do_p, do_q):
        before_p = p_m if t == 0 else p[t - 1]
        before_q = q_m if t == 0 else q[t - 1]
        off = 0 if t == 0 else 4
        y0 = 0 if t == 0 else 8
        last = t == STEPS - 1

        def plane(x):
            k = lax.rem(x + shift, N)
            amount = jnp.where(x + gx * N == sources[0, 0], wavelet[0, t], jnp.float32(0))
            for half in range(2):
                h = lap[x, half] if t == 0 else laplace(t, x, half)
                z = deep[x, half]
                b = gain_b[k, half]
                if do_p:
                    new_p = (2.0 * p[t][x + 4, half, 8:40, :] - before_p[x + off, half, y0:y0 + N, :]) + (
                        gain_a[k, half] * h + b * z)
                    new_p = new_p + amount * spot[half]
                    if last:
                        p_out[0, x, :, 128 * half:128 * half + 128] = new_p
                    else:
                        p[t + 1][x + 4, half, 8:40, :] = new_p
                    if t == 0:
                        stage[0, half, pl.ds(x, 4, stride=N), :] = new_p[0:4]
                        stage[1, half, pl.ds(x, 4, stride=N), :] = new_p[28:32]
                if do_q:
                    new_q = (2.0 * q[t][x, half] - before_q[x, half]) + (b * h + gain_c[k, half] * z)
                    if last:
                        q_out[0, x, :, 128 * half:128 * half + 128] = new_q
                    else:
                        q[t + 1][x, half] = new_q

        @pl.loop(0, N // 2)
        def _(pair):
            plane(2 * pair)
            plane(2 * pair + 1)

    def bump_p(t, x, k, half, first, count, value):
        rows = slice(first, first + count)
        add = gain_a[k, half, rows, :] * value
        if t == STEPS - 1:
            z = slice(128 * half, 128 * half + 128)
            p_out[0, x, rows, z] = p_out[0, x, rows, z] + add
        else:
            lower = slice(8 + first, 8 + first + count)
            new_p = p[t + 1][x + 4, half, lower, :] + add
            p[t + 1][x + 4, half, lower, :] = new_p

    def bump_q(t, x, k, half, first, count, value):
        rows = slice(first, first + count)
        add = gain_b[k, half, rows, :] * value
        if t == STEPS - 1:
            z = slice(128 * half, 128 * half + 128)
            q_out[0, x, rows, z] = q_out[0, x, rows, z] + add
        else:
            q[t + 1][x, half, rows, :] = q[t + 1][x, half, rows, :] + add

    def add_x(t, bumps):
        for side in range(2):
            for half in range(2):
                for i, value in enumerate(corrections(unpack_layers(x_in.at[t, side, half], side), side)):
                    x = 28 * side + i
                    for bump in bumps:
                        bump(t, x, lax.rem(x + shift, N), half, 0, N, value)

    def add_y(t, bumps, halves):
        @pl.loop(0, N // 4)
        def _(pair):
            for u in range(4):
                x = 4 * pair + u
                k = lax.rem(x + shift, N)
                for half in halves:
                    for side in range(2):
                        value = corner[side, half, pl.ds(x, 4, stride=N), :]
                        for bump in bumps:
                            bump(t, x, k, half, 28 * side, 4, value)

    def each_rim(move, first, last):
        @pl.loop(first, last)
        def _(x):
            for half in range(2):
                for side in range(2):
                    move(x, half, side)

    def keep_gain(x, half, side):
        face[side, half, pl.ds(x, 4, stride=N), :] = gain_a[lax.rem(x + shift, N), half, 28 * side:28 * side + 4, :]

    def pass_on(t):
        def give(x, half, side):
            p[t + 1][x + 4, half, 8 + 28 * side:12 + 28 * side, :] = stage[side, half, pl.ds(x, 4, stride=N), :]

        for half in range(2):
            await_y(t, half)
            for side in range(2):
                stage[side, half] = stage[side, half] + face[side, half] * corner[side, half]
            send_y(t + 1, half)
        each_rim(give, 0, 4)
        each_rim(give, 28, 32)
        send_x(t + 1)
        each_rim(give, 4, 28)

    step(0, True, False)
    each_rim(keep_gain, 0, N)
    pass_on(0)
    step(0, False, True)
    add_y(0, (bump_q,), (0, 1))
    for t in range(1, STEPS):
        depth_term(t)
        step(t, True, True)
        await_x(t)
        add_x(t, (bump_p, bump_q))
        if t == STEPS - 1:
            for half in range(2):
                await_y(t, half)
                add_y(t, (bump_p, bump_q), (half,))
            break

        def take(x, half, side):
            stage[side, half, pl.ds(x, 4, stride=N), :] = p[t + 1][x + 4, half, 8 + 28 * side:12 + 28 * side, :]

        each_rim(take, 0, N)
        pass_on(t)
        add_y(t, (bump_q,), (0, 1))

    for side in range(2):
        @pl.when(has_gx[side])
        def _():
            for t in range(STEPS):
                x_halo(t, side).wait_send()

        @pl.when(has_gy[side])
        def _():
            for t in range(STEPS):
                y_halo(t, side, 0).wait_send()
                y_halo(t, side, 1).wait_send()

    for c in range(CHUNKS):
        for slot, (other, hop) in enumerate(PARTNERS):
            spread[c, other, hop].wait_send()
            deal[c, slot].wait_send()
        for piece in range(5):
            x_copy[c, piece].wait_send()


def keep(p_in, q_in, p_out, q_out, sem):
    copies = [pltpu.make_async_copy(p_in, p_out, sem.at[0]), pltpu.make_async_copy(q_in, q_out, sem.at[1])]
    for copy in copies:
        copy.start()
    for copy in copies:
        copy.wait()


def on_device(velocity, epsilon, delta, anchors, sources, wavelet, p_now, p_prev, q_now, q_prev):
    out = pltpu.VMEM(p_now.shape, jnp.float32)
    vmem = pl.BlockSpec(memory_space=pltpu.VMEM)
    hbm = pl.BlockSpec(memory_space=pl.ANY)
    smem = pl.BlockSpec(memory_space=pltpu.SMEM)
    f32 = jnp.float32
    bf16 = jnp.bfloat16
    block = pltpu.VMEM((N, 2, N, 128), f32)
    padded = pltpu.VMEM((N + 8, 2, N + 16, 128), f32)
    rims = pltpu.VMEM((STEPS, 2, 2, 5, N, 128), bf16)
    dma = pltpu.SemaphoreType.DMA
    p_end, q_end = pl.pallas_call(
        kernel,
        out_shape=(out, out),
        in_specs=[hbm, hbm, hbm, smem, smem, smem, hbm, hbm, hbm, hbm],
        out_specs=(vmem, vmem),
        scratch_shapes=[
            pltpu.VMEM((3, N, N, 256), bf16),
            *[pltpu.VMEM((4, 4, models, count, 256), bf16) for _, _, count, _, models in PIECES],
            pltpu.VMEM((7, 3, 4, N, 256), bf16),
            pltpu.VMEM((3, 4, 8, N, 256), bf16),
            block, block, block, block, block,
            pltpu.VMEM((256, 256), bf16), pltpu.VMEM((256, 256), bf16), pltpu.VMEM((2, N, 128), f32),
            block, padded, padded, padded, padded,
            block, block, block, block, block,
            pltpu.VMEM((2, 2, 4 * N, 128), f32), pltpu.VMEM((2, 2, 4 * N, 128), f32), pltpu.VMEM((2, 2, 4 * N, 128), f32),
            rims, rims, rims, rims,
            dma((11,)), dma((CHUNKS, 2, 4)), dma((CHUNKS, 2, 4)), dma((CHUNKS,)), dma((CHUNKS, 5)), dma((CHUNKS, 5)),
            dma((CHUNKS, 7)), dma((CHUNKS, 7)),
            dma((STEPS, 6)), dma((STEPS, 6)),
        ],
        compiler_params=pltpu.CompilerParams(
            collective_id=0, has_side_effects=True, vmem_limit_bytes=56 << 20),
        name="migrate",
    )(velocity, epsilon, delta, anchors, sources, wavelet, p_now, p_prev, q_now, q_prev)
    result = jax.ShapeDtypeStruct(p_now.shape, f32)
    return pl.pallas_call(
        keep,
        out_shape=(result, result),
        in_specs=[vmem, vmem],
        out_specs=(hbm, hbm),
        scratch_shapes=[dma((2,))],
        name="keep",
    )(pltpu.with_memory_space_constraint(p_end, pltpu.VMEM), pltpu.with_memory_space_constraint(q_end, pltpu.VMEM))


def solution(mesh):
    field = P("shot", "gx", "gy", None)
    model = P(("shot", "gx"), "gy", None)
    return jax.shard_map(
        on_device,
        mesh=mesh,
        in_specs=(model, model, model, P(), P("shot", None), P("shot", None), field, field, field, field),
        out_specs=(field, field),
        check_vma=False,
    )
```
